128 devices in a mesh: seq: 64 (over x, z, y), mp: 2 (over core).
Axes of the slice: x: 4, y: 4, z: 4, core: 2. Of those that a mesh axis runs over, the one named last changes fastest.
Arguments:
- tokens: bfloat16 [8192, 2688], P('seq'), may hold values from -16 to 16
- tangent: bfloat16 [8192, 2688], P('seq'), may hold values from -6 to 6
- w_query: bfloat16 [2688, 2048], P(None, 'mp'), may hold values from -0.078116071 to 0.078116071
- w_key: bfloat16 [2688, 1024], P(None, 'mp'), may hold values from -0.078116071 to 0.078116071
- value_weight: bfloat16 [2688, 1024], P(None, 'mp'), may hold values from -0.125 to 0.125
- w_out: bfloat16 [2048, 2688], P('mp'), may hold values from -0.125 to 0.125
Outputs:
- input_grad: bfloat16 [8192, 2688], P('seq', 'mp')
- weight_grad: float32 [2688, 2, 1024], P('seq', None, 'mp')
The draws below stay inside these ranges and needn't reach their ends.
All inputs are finite; a program needn't handle non-finite values.
Results may differ from the reference program's by a relative error of at most 0.011.
Values may be sent and summed in bfloat16 or wider, within the bound.
No kernel may reach another device: no remote copies, remote signals or barrier semaphores. Data moves between devices by JAX's collectives and lax.ppermute only.
A program may use at most 128 MiB of HBM per device.

```python
import math
import jax
import jax.numpy as jnp
from jax import lax

MODEL_WIDTH = 2688
QUERY_HEADS = 16
KEY_VALUE_HEADS = 8
HEAD_SIZE = 128
WINDOW = 1024
TOKENS_PER_PART = 128
TOKENS = 8192


def query_value_rows(key):
    normal_values = jax.random.normal(jax.random.fold_in(key, 11), (MODEL_WIDTH, QUERY_HEADS * HEAD_SIZE), jnp.float32)
    return jnp.clip(normal_values, -4.0, 4.0) * MODEL_WIDTH ** (-0.5)


def draw_w_query(key, part):
    return query_value_rows(key).astype(jnp.bfloat16)


def draw_w_key(key, part):
    new_partial = jnp.clip(jax.random.normal(jax.random.fold_in(key, 12), (MODEL_WIDTH, KEY_VALUE_HEADS * HEAD_SIZE), jnp.float32), -4.0, 4.0) * MODEL_WIDTH ** (-0.5)
    return new_partial.astype(jnp.bfloat16)


def draw_tokens(key, part):
    base_values = jnp.clip(jax.random.normal(jax.random.fold_in(key, 21), (TOKENS, MODEL_WIDTH), jnp.float32), -5.0, 5.0)
    row_scales = jnp.exp(jax.random.uniform(jax.random.fold_in(key, 23), (TOKENS, 1), jnp.float32, math.log(0.5), math.log(3.0)))
    values = base_values * row_scales
    return jnp.clip(values, -16.0, 16.0).astype(jnp.bfloat16)


def level_of(stream_key, shape, shards, least, top_value):
    level = 1.0
    for position, parts in shards:
        steps = jax.random.uniform(jax.random.fold_in(jax.random.fold_in(stream_key, 6), position), (parts,), jnp.float32, least / len(shards), top_value / len(shards))
        level = level * jnp.repeat(jnp.exp(steps), shape[position] // parts).reshape((-1,) + (1,) * (len(shape) - 1 - position))
    return level


def bell_draw(own_key, extent, spread, most, pieces=(), kind=jnp.bfloat16):
    entries = spread * jax.random.normal(own_key, extent, jnp.float32)
    if pieces:
        entries = entries * level_of(own_key, extent, pieces, -0.22, 0.18)
    return jnp.clip(entries, -most, most).astype(kind)


def setup_inputs(seed: int = 0) -> dict:
    key_list = jax.random.split(jax.random.key(seed), 7)
    return {
        "tokens": draw_tokens(jax.random.fold_in(key_list[6], 71), 0),
        "tangent": bell_draw(key_list[1], (TOKENS, MODEL_WIDTH), 1.0, 6.0, ((0, 64),)),
        "w_query": draw_w_query(jax.random.fold_in(key_list[6], 71), 0),
        "w_key": draw_w_key(jax.random.fold_in(key_list[6], 71), 0),
        "value_weight": bell_draw(key_list[4], (MODEL_WIDTH, KEY_VALUE_HEADS * HEAD_SIZE), MODEL_WIDTH ** -0.5, 0.125, ((1, 2),)),
        "w_out": bell_draw(key_list[5], (QUERY_HEADS * HEAD_SIZE, MODEL_WIDTH), (QUERY_HEADS * HEAD_SIZE) ** -0.5, 0.125, ((0, 2),)),
    }


score_scale = 168.0 ** -0.5


def probabilities(raw_scores, allowed):
    scaled = jnp.where(allowed, raw_scores * score_scale, -1e30)
    highest = jnp.max(scaled, axis=-1, keepdims=True)
    weights = jnp.exp(scaled - highest)
    return weights / jnp.sum(weights, axis=-1, keepdims=True)


def rounded(values):
    return lax.optimization_barrier(values.astype(jnp.bfloat16)).astype(jnp.float32)


def project(rows_in, weight):
    return jnp.dot(rows_in, weight, preferred_element_type=jnp.float32).astype(jnp.bfloat16)


def reference(tokens, tangent, w_query, w_key, value_weight, w_out):
    token_total = tokens.shape[0]
    block_count = token_total // TOKENS_PER_PART
    group_width = QUERY_HEADS // KEY_VALUE_HEADS
    pair_length = KEY_VALUE_HEADS * HEAD_SIZE
    key_extent = WINDOW + TOKENS_PER_PART
    query_matrix = project(tokens, w_query)
    query_tangent = project(tangent, w_query)
    padding = jnp.zeros((WINDOW, pair_length), jnp.bfloat16)
    key_projected = jnp.stack([
        jnp.concatenate([padding, project(tokens, w_key)], axis=0),
        jnp.concatenate([padding, project(tokens, value_weight)], axis=0),
        jnp.concatenate([padding, project(tangent, w_key)], axis=0),
        jnp.concatenate([padding, project(tangent, value_weight)], axis=0)])

    def gather_block(block_index):
        opening_row = (block_index * TOKENS_PER_PART).astype(jnp.int32)
        query_head_rows = lax.dynamic_slice_in_dim(query_matrix, opening_row, TOKENS_PER_PART, 0).astype(jnp.float32).reshape(TOKENS_PER_PART, KEY_VALUE_HEADS, group_width, HEAD_SIZE)
        query_tangent_heads = lax.dynamic_slice_in_dim(query_tangent, opening_row, TOKENS_PER_PART, 0).astype(jnp.float32).reshape(TOKENS_PER_PART, KEY_VALUE_HEADS, group_width, HEAD_SIZE)
        neighbour_keys = lax.dynamic_slice_in_dim(key_projected, opening_row, key_extent, 1).astype(jnp.float32).reshape(4, key_extent, KEY_VALUE_HEADS, HEAD_SIZE)
        q_pos = opening_row + jnp.arange(TOKENS_PER_PART, dtype=jnp.int32)
        k_pos = opening_row - WINDOW + jnp.arange(key_extent, dtype=jnp.int32)
        distance = q_pos[:, None] - k_pos[None, :]
        allowed = (distance >= 0) & (distance < WINDOW) & (k_pos[None, :] >= 0)
        attend = probabilities(jnp.einsum("tgjd,sgd->gjts", query_head_rows, neighbour_keys[0]), allowed)
        return query_head_rows, query_tangent_heads, neighbour_keys, attend, opening_row

    def forward_block(block_index):
        query_head_rows, query_tangent_heads, neighbour_keys, attend, opening_row = gather_block(block_index)
        score_dot = score_scale * (jnp.einsum("tgjd,sgd->gjts", query_tangent_heads, neighbour_keys[0]) + jnp.einsum("tgjd,sgd->gjts", query_head_rows, neighbour_keys[2]))
        attend_dot = attend * (score_dot - jnp.sum(attend * score_dot, axis=-1, keepdims=True))
        mixed_dot = jnp.einsum("gjts,sgd->tgjd", rounded(attend_dot), neighbour_keys[1]) + jnp.einsum("gjts,sgd->tgjd", rounded(attend), neighbour_keys[3])
        return mixed_dot.astype(jnp.bfloat16).reshape(TOKENS_PER_PART, QUERY_HEADS * HEAD_SIZE)

    mixed_all = lax.map(forward_block, jnp.arange(block_count, dtype=jnp.int32)).reshape(token_total, QUERY_HEADS * HEAD_SIZE)
    cotangent = project(mixed_all, w_out)
    output_gradient = project(cotangent, w_out.T)

    def backward_block(buffer, block_index):
        query_head_rows, query_tangent_heads, neighbour_keys, attend, opening_row = gather_block(block_index)
        gradient_heads = lax.dynamic_slice_in_dim(output_gradient, opening_row, TOKENS_PER_PART, 0).astype(jnp.float32).reshape(TOKENS_PER_PART, KEY_VALUE_HEADS, group_width, HEAD_SIZE)
        attend_grad = jnp.einsum("tgjd,sgd->gjts", gradient_heads, neighbour_keys[1])
        score_grad = rounded(attend * (attend_grad - jnp.sum(attend * attend_grad, axis=-1, keepdims=True)))
        query_grad = (score_scale * jnp.einsum("gjts,sgd->tgjd", score_grad, neighbour_keys[0])).astype(jnp.bfloat16).reshape(TOKENS_PER_PART, QUERY_HEADS * HEAD_SIZE)
        key_partial = score_scale * jnp.einsum("gjts,tgjd->sgd", score_grad, query_head_rows)
        value_partial = jnp.einsum("gjts,tgjd->sgd", rounded(attend), gradient_heads)
        partial_value = jnp.stack([key_partial, value_partial]).reshape(2, key_extent, pair_length)
        existing = lax.dynamic_slice_in_dim(buffer, opening_row, key_extent, 1)
        buffer = lax.dynamic_update_slice_in_dim(buffer, existing + partial_value, opening_row, 1)
        return buffer, query_grad

    start_buffer = jnp.zeros((2, WINDOW + token_total, pair_length), jnp.float32)
    summed, query_grads = lax.scan(backward_block, start_buffer, jnp.arange(block_count, dtype=jnp.int32))
    query_grads = query_grads.reshape(token_total, QUERY_HEADS * HEAD_SIZE)
    key_grad = summed[0, WINDOW:].astype(jnp.bfloat16)
    value_grad = summed[1, WINDOW:].astype(jnp.bfloat16)
    input_terms = jnp.dot(query_grads, w_query.T, preferred_element_type=jnp.float32)
    input_terms = input_terms + jnp.dot(key_grad, w_key.T, preferred_element_type=jnp.float32)
    input_terms = input_terms + jnp.dot(value_grad, value_weight.T, preferred_element_type=jnp.float32)
    input_grad = input_terms.astype(jnp.bfloat16)
    pair_grad = jnp.concatenate([key_grad, value_grad], axis=1)
    weight_grad = jnp.dot(tokens.T, pair_grad, preferred_element_type=jnp.float32).reshape(MODEL_WIDTH, 2, pair_length)
    return input_grad, weight_grad
```

```python
import functools
import math

import jax
import jax.numpy as jnp
from jax import lax
from jax.experimental import pallas as pl
from jax.experimental.pallas import tpu as pltpu
from jax.sharding import PartitionSpec as P

BF = jnp.bfloat16
F32 = jnp.float32
HEAD = 128
LINE = 4
SCALE = 168.0 ** (-0.5)
SCALE2 = SCALE * math.log2(math.e)
PIECE = 48


NT = (((1,), (1,)), ((), ()))
TN = (((0,), (0,)), ((), ()))
NN = (((1,), (0,)), ((), ()))


def mm(a, b, dims=NN):
    return lax.dot_general(a, b, dims, preferred_element_type=F32)


def ring_y(x, d):
    return lax.ppermute(x, "seq", [(i, i // 4 * 4 + (i + d) % 4) for i in range(64)])


def ring_z(x, d):
    return lax.ppermute(
        x, "seq", [(i, i // 16 * 16 + (i // 4 + d) % 4 * 4 + i % 4) for i in range(64)]
    )


def ring_x(x, d):
    return lax.ppermute(x, "seq", [(i, (i // 16 + d) % 4 * 16 + i % 16) for i in range(64)])


def lines_on(x, d):
    return lax.ppermute(x, "seq", [(i, i + 4 * d) for i in range(64) if 0 <= i + 4 * d < 64])


def other_core(x):
    return lax.ppermute(x, "mp", [(0, 1), (1, 0)])


def call(kernel, grid, ins, outs, scratch=(), flops=0, moved=0):
    specs_in, values = zip(*ins[1:])
    specs_out, shapes = zip(*outs)
    return pl.pallas_call(
        kernel,
        grid_spec=pltpu.PrefetchScalarGridSpec(
            num_scalar_prefetch=1,
            grid=grid,
            in_specs=list(specs_in),
            out_specs=list(specs_out),
            scratch_shapes=list(scratch),
        ),
        out_shape=list(shapes),
        compiler_params=pltpu.CompilerParams(
            dimension_semantics=("arbitrary",) * len(grid), vmem_limit_bytes=48 << 20
        ),
        cost_estimate=pl.CostEstimate(flops=flops, bytes_accessed=moved, transcendentals=0),
    )(ins[0], *values)


def whole(shape):
    return pl.BlockSpec(shape, lambda *_: (0,) * len(shape))


def hbm():
    return pl.BlockSpec(memory_space=pl.ANY)


def out(shape, dtype):
    return whole(shape), jax.ShapeDtypeStruct(shape, dtype)


def key_value_kernel(pos, tok, tan, wk, wv, *outs):
    step = pl.program_id(0)
    k = mm(tok[...], wk[...])
    v = mm(tok[...], wv[...])
    kd = mm(tan[...], wk[...])
    vd = mm(tan[...], wv[...])
    for d in range(4):

        @pl.when(step == d)
        def _():
            outs[d][0] = k.astype(BF)
            outs[d][1] = kd.astype(BF)
            outs[d][2] = v.astype(BF)
            outs[d][3] = vd.astype(BF)


def query_kernel(pos, tok, tan, w, *outs):
    step = pl.program_id(0)
    q = mm(tok[...], w[...])
    qd = mm(tan[...], w[...])
    for d in range(4):

        @pl.when(step == d)
        def _():
            outs[d][0] = q.astype(BF)
            outs[d][1] = qd.astype(BF)


def two_heads(block):
    return jnp.concatenate([block[:, :HEAD], block[:, HEAD:]], axis=0)


def forward_kernel(pos, *refs):
    kv_refs = refs[:12]
    q_refs = refs[12:16]
    o0, o1, o2, o3, k_all, v_all, q_all, p_all, kkd, vvd, qbuf, sems = refs[16:]
    outs = (o0, o1, o2, o3)
    b = pl.program_id(0)
    y = pos[2]

    @pl.when(b == 0)
    def _():
        copies = []
        for line in range(3):
            for d in range(4):
                row = pl.multiple_of((lax.rem(y + 4 - d, 4) + 4 * line) * HEAD, HEAD)
                src = kv_refs[line * 4 + d]
                for part in range(4):
                    dst = kkd if part < 2 else vvd
                    copies.append(
                        pltpu.make_async_copy(
                            src.at[part],
                            dst.at[pl.ds(row, HEAD), pl.ds(part % 2 * HEAD, HEAD)],
                            sems.at[line * 16 + d * 4 + part],
                        )
                    )
        for d in range(4):
            copies.append(
                pltpu.make_async_copy(
                    q_refs[d], qbuf.at[lax.rem(y + 4 - d, 4)], sems.at[48 + d]
                )
            )
        for c in copies:
            c.start()
        for c in copies:
            c.wait()
        k_all[...] = kkd[:, :HEAD]
        v_all[...] = vvd[:, :HEAD]

    rows = pl.ds(pl.multiple_of(b * HEAD, HEAD), 9 * HEAD)
    q = two_heads(qbuf[b, 0])
    qd = two_heads(qbuf[b, 1])
    q_all[0] = q
    keys = kkd[rows, :]
    s = mm(keys[:, :HEAD], q, NT)
    u = lax.broadcasted_iota(jnp.int32, s.shape, 0)
    t = lax.rem(lax.broadcasted_iota(jnp.int32, (1, s.shape[1]), 1), HEAD)
    first = 1024 - b * HEAD - 512 * (4 * pos[0] + pos[1])
    allowed = (u >= jnp.maximum(t + 1, first)) & (u <= t + 1024)
    s = jnp.where(allowed, s, -1e30)
    e = jnp.exp2((s - jnp.max(s, axis=0, keepdims=True)) * SCALE2)
    inv = 1.0 / jnp.sum(e, axis=0, keepdims=True)
    sd = mm(keys, jnp.concatenate([qd, q], axis=1), NT)
    mean = jnp.sum(e * sd, axis=0, keepdims=True) * inv
    p_b = (e * inv).astype(BF)
    pd_b = (e * ((sd - mean) * (inv * SCALE))).astype(BF)
    p_all[0] = p_b
    values = vvd[rows, :]
    mixed = mm(values[:, :HEAD], pd_b, TN) + mm(values[:, HEAD:], p_b, TN)
    mixed = jnp.concatenate([mixed[:, :HEAD].T, mixed[:, HEAD:].T], axis=1).astype(BF)
    target = lax.rem(b + 4 - y, 4)
    for d in range(4):

        @pl.when(target == d)
        def _():
            outs[d][...] = mixed


def out_kernel(pos, o0, o1, o2, o3, w, total, sent, acc):
    step = pl.program_id(0)
    for d, o in enumerate((o0, o1, o2, o3)):

        @pl.when(step == d)
        def _():
            part = mm(o[...], w[...])
            if d == 0:
                acc[...] = part
            elif d < 3:
                acc[...] += part
            else:
                full = acc[...] + part
                total[...] = full
                sent[...] = full.astype(BF)


def gradient_kernel(pos, total, other, w, g0, g1, g2, g3, ct):
    step = pl.program_id(0)

    @pl.when(step == 0)
    def _():
        ct[...] = (total[...] + other[...].astype(F32)).astype(BF)

    g = mm(ct[...], w[...], NT).astype(BF)
    for d, ref in enumerate((g0, g1, g2, g3)):

        @pl.when(step == d)
        def _():
            ref[...] = g


def backward_kernel(pos, g0, g1, g2, g3, k_all, v_all, q_all, p_all, *refs):
    q0, q1, q2, q3, own, near, far, dk, dv = refs
    b = pl.program_id(0)
    y = pos[2]
    source = lax.rem(y + 4 - b, 4)
    target = lax.rem(b + 4 - y, 4)

    @pl.when(b == 0)
    def _():
        dk[...] = jnp.zeros_like(dk)
        dv[...] = jnp.zeros_like(dv)

    g = jnp.where(
        source < 2,
        jnp.where(source == 0, g0[...], g1[...]),
        jnp.where(source == 2, g2[...], g3[...]),
    )
    g = two_heads(g)
    rows = pl.ds(pl.multiple_of(b * HEAD, HEAD), 9 * HEAD)
    keys = k_all[rows, :]
    p_b = p_all[0]
    q = q_all[0]
    dp = mm(v_all[rows, :], g, NT)
    p = p_b.astype(F32)
    ds = (p * (dp - jnp.sum(p * dp, axis=0, keepdims=True))).astype(BF)
    dq = mm(keys, ds, TN) * SCALE
    dq = jnp.concatenate([dq[:, :HEAD].T, dq[:, HEAD:].T], axis=1).astype(BF)
    for d, ref in enumerate((q0, q1, q2, q3)):

        @pl.when(target == d)
        def _():
            ref[...] = dq

    dk[rows, :] += mm(ds, q)
    dv[rows, :] += mm(p_b, g)

    @pl.when(b == 3)
    def _():
        far[:, :HEAD] = (dk[:512, :] * SCALE).astype(BF)
        far[:, HEAD:] = dv[:512, :].astype(BF)
        near[:, :HEAD] = (dk[512:1024, :] * SCALE).astype(BF)
        near[:, HEAD:] = dv[512:1024, :].astype(BF)
        own[:, :HEAD] = dk[1024:, :] * SCALE
        own[:, HEAD:] = dv[1024:, :]


def pair_kernel(pos, own, near, far, *outs):
    y = pos[2]
    for d in range(4):
        rows = pl.ds(pl.multiple_of(lax.rem(y + d, 4) * HEAD, HEAD), HEAD)
        outs[d][...] = (
            own[rows, :] + near[rows, :].astype(F32) + far[rows, :].astype(F32)
        ).astype(BF)


def query_input_kernel(pos, q0, q1, q2, q3, w, total, acc):
    step = pl.program_id(0)
    for d, q in enumerate((q0, q1, q2, q3)):

        @pl.when(step == d)
        def _():
            part = mm(q[...], w[...], NT)
            if d == 0:
                acc[...] = part
            elif d < 3:
                acc[...] += part
            else:
                total[...] = acc[...] + part


def pair_input_kernel(pos, c0, c1, c2, c3, base, wk, wv, total, acc):
    step = pl.program_id(0)
    for d, c in enumerate((c0, c1, c2, c3)):

        @pl.when(step == d)
        def _():
            part = mm(c[:, :HEAD], wk[...], NT) + mm(c[:, HEAD:], wv[...], NT)
            if d == 0:
                acc[...] = base[...] + part
            elif d < 3:
                acc[...] += part
            else:
                total[...] = acc[...] + part


def weight_kernel(pos, *refs):
    mine, r1, r2, r3, p1, p2, p3, c0, c1, c2, c3 = refs[:11]
    a_outs = refs[11:15]
    b_outs = refs[15:19]
    line, sems = refs[19:]
    core = pos[3]
    half = r1.shape[0]
    copies = [pltpu.make_async_copy(mine, line.at[:, pl.ds(0, HEAD)], sems.at[0])]
    for d, (r, p) in enumerate(((r1, p1), (r2, p2), (r3, p3)), 1):
        for j, (src, where) in enumerate(((r, core), (p, 1 - core))):
            rows = pl.ds(pl.multiple_of(where * half, half), half)
            copies.append(
                pltpu.make_async_copy(
                    src, line.at[rows, pl.ds(d * HEAD, HEAD)], sems.at[2 * d - 1 + j]
                )
            )
    for c in copies:
        c.start()
    for c in copies:
        c.wait()
    pair = jnp.concatenate([c0[...], c3[...], c2[...], c1[...]], axis=0)
    size = 4 * PIECE
    for d in range(4):
        for e in range(4):
            x, z = lax.rem(pos[0] + d, 4), e
            block = line[pl.ds(pl.multiple_of((4 * x + z) * size, size), size), :]
            a_outs[d][e * size : (e + 1) * size, :] = mm(block, pair[:, :HEAD]).astype(BF)
            x, z = e, lax.rem(pos[1] + d, 4)
            block = line[pl.ds(pl.multiple_of((4 * x + z) * size, size), size), :]
            b_outs[d][e * size : (e + 1) * size, :] = mm(block, pair[:, HEAD:]).astype(BF)


def middle_kernel(pos, *refs):
    a_in, b_in, a_out, b_out = refs[:4], refs[4:8], refs[8:12], refs[12:16]
    size = 4 * PIECE
    for ins, outs, at in ((a_in, a_out, pos[1]), (b_in, b_out, pos[0])):
        for d in range(4):
            rows = pl.ds(pl.multiple_of(lax.rem(at + d, 4) * size, size), size)
            total = ins[0][rows, :].astype(F32)
            for r in ins[1:]:
                total += r[rows, :].astype(F32)
            outs[d][...] = total.astype(BF)


def last_kernel(pos, *refs):
    a_in, b_in, outs = refs[:4], refs[4:8], refs[8:12]
    for d in range(4):
        rows = pl.ds(pl.multiple_of(lax.rem(pos[2] + d, 4) * PIECE, PIECE), PIECE)
        for j, ins in enumerate((a_in, b_in)):
            total = ins[0][rows, :].astype(F32)
            for r in ins[1:]:
                total += r[rows, :].astype(F32)
            outs[d][:, j * HEAD : (j + 1) * HEAD] = total


def place_kernel(pos, c0, c1, c2, c3, res):
    for d, c in enumerate((c0, c1, c2, c3)):
        head = pl.multiple_of(lax.rem(pos[2] + 4 - d, 4) * HEAD, HEAD)
        for j in range(2):
            res[:, j, pl.ds(head, HEAD)] = c[: res.shape[0], j * HEAD : (j + 1) * HEAD]


def on_device(tokens, tangent, w_query, w_key, value_weight, w_out):
    rows, width = tokens.shape
    seq = lax.axis_index("seq")
    core = lax.axis_index("mp")
    pos = jnp.stack([seq // 16, seq // 4 % 4, seq % 4, core]).astype(jnp.int32)
    piece_out = [out((4, rows, HEAD), BF)] * 4

    def column(d_sign, size):
        return pl.BlockSpec((width, size), lambda i, p: (0, lax.rem(p[2] + 4 + d_sign * i, 4)))

    def row(d_sign, size):
        return pl.BlockSpec((size, width), lambda i, p: (lax.rem(p[2] + 4 + d_sign * i, 4), 0))

    tok_in = (whole((rows, width)), tokens)
    tan_in = (whole((rows, width)), tangent)
    kv = call(
        key_value_kernel,
        (4,),
        [pos, tok_in, tan_in, (column(1, HEAD), w_key), (column(1, HEAD), value_weight)],
        piece_out,
        flops=2 * 256 * width * 1024,
        moved=2 * width * 1024,
    )
    line = [kv[0]] + [ring_y(kv[d], d) for d in range(1, 4)]
    near = [lines_on(c, 1) for c in line]
    far = [lines_on(c, 2) for c in line]

    q = call(
        query_kernel,
        (4,),
        [pos, tok_in, tan_in, (column(1, 256), w_query)],
        [out((2, rows, 256), BF)] * 4,
        flops=2 * 256 * width * 1024,
        moved=2 * width * 1024,
    )
    q = [q[0]] + [ring_y(q[d], d) for d in range(1, 4)]

    columns = jnp.pad(tokens.reshape(rows, 64, width // 64), ((0, 0), (0, 0), (0, PIECE - width // 64)))
    columns = columns.reshape(rows, 64 * PIECE).T
    half = lax.dynamic_slice_in_dim(columns, core * (32 * PIECE), 32 * PIECE, 0)
    halves = [ring_y(half, d) for d in range(1, 4)]
    partner_halves = [other_core(h) for h in halves]

    attended = call(
        forward_kernel,
        (4,),
        [pos] + [(hbm(), a) for a in far + near + line + q],
        [out((rows, 256), BF)] * 4
        + [
            out((1536, HEAD), BF),
            out((1536, HEAD), BF),
            (pl.BlockSpec((1, 256, HEAD), lambda i, p: (i, 0, 0)), jax.ShapeDtypeStruct((4, 256, HEAD), BF)),
            (pl.BlockSpec((1, 1152, 256), lambda i, p: (i, 0, 0)), jax.ShapeDtypeStruct((4, 1152, 256), BF)),
        ],
        [
            pltpu.VMEM((1536, 256), BF),
            pltpu.VMEM((1536, 256), BF),
            pltpu.VMEM((4, 2, rows, 256), BF),
            pltpu.SemaphoreType.DMA((52,)),
        ],
        flops=2 * 4 * 1152 * 256 * 128 * 5,
        moved=8 << 20,
    )
    o, (k_all, v_all, q_all, p_all) = attended[:4], attended[4:]
    o = [o[0]] + [ring_y(o[d], d) for d in range(1, 4)]
    small = whole((rows, 256))
    full = whole((rows, width))
    total, sent = call(
        out_kernel,
        (4,),
        [pos] + [(small, a) for a in o] + [(row(-1, 256), w_out)],
        [out((rows, width), F32), out((rows, width), BF)],
        [pltpu.VMEM((rows, width), F32)],
        flops=2 * rows * width * 1024,
        moved=2 * width * 1024,
    )
    other = other_core(sent)
    g = call(
        gradient_kernel,
        (4,),
        [pos, (full, total), (full, other), (row(1, 256), w_out)],
        [out((rows, 256), BF)] * 4,
        [pltpu.VMEM((rows, width), BF)],
        flops=2 * rows * width * 1024,
        moved=2 * width * 1024,
    )
    g = [g[0]] + [ring_y(g[d], d) for d in range(1, 4)]
    back = call(
        backward_kernel,
        (4,),
        [pos]
        + [(small, a) for a in g]
        + [
            (whole((1536, HEAD)), k_all),
            (whole((1536, HEAD)), v_all),
            (pl.BlockSpec((1, 256, HEAD), lambda i, p: (i, 0, 0)), q_all),
            (pl.BlockSpec((1, 1152, 256), lambda i, p: (i, 0, 0)), p_all),
        ],
        [out((rows, 256), BF)] * 4 + [out((512, 256), F32), out((512, 256), BF), out((512, 256), BF)],
        [pltpu.VMEM((1536, HEAD), F32), pltpu.VMEM((1536, HEAD), F32)],
        flops=2 * 4 * 1152 * 256 * 128 * 4,
        moved=6 << 20,
    )
    dq, (own, to_near, to_far) = back[:4], back[4:]
    from_near = lines_on(to_near, -1)
    from_far = lines_on(to_far, -2)
    dq = [dq[0]] + [ring_y(dq[d], d) for d in range(1, 4)]
    (base,) = call(
        query_input_kernel,
        (4,),
        [pos] + [(small, a) for a in dq] + [(column(-1, 256), w_query)],
        [out((rows, width), F32)],
        [pltpu.VMEM((rows, width), F32)],
        flops=2 * rows * width * 1024,
        moved=2 * width * 1024,
    )
    pair = call(
        pair_kernel,
        (1,),
        [pos] + [(whole((512, 256)), a) for a in (own, from_near, from_far)],
        [out((rows, 256), BF)] * 4,
        moved=1 << 20,
    )
    mixed_pair = [pair[0]] + [ring_y(pair[d], d) for d in range(1, 4)]

    third = (48 * 16, HEAD)
    stage = call(
        weight_kernel,
        (1,),
        [pos] + [(hbm(), a) for a in [columns] + halves + partner_halves] + [(small, a) for a in pair],
        [out(third, BF)] * 8,
        [pltpu.VMEM((64 * PIECE, 512), BF), pltpu.SemaphoreType.DMA((7,))],
        flops=2 * 3072 * 512 * 256,
        moved=5 << 20,
    )
    a, b = stage[:4], stage[4:]
    a = [a[0]] + [ring_x(a[d], d) for d in range(1, 4)]
    b = [b[0]] + [ring_z(b[d], d) for d in range(1, 4)]
    quarter = (4 * PIECE, HEAD)
    stage = call(
        middle_kernel,
        (1,),
        [pos] + [(whole(third), v) for v in a + b],
        [out(quarter, BF)] * 8,
        moved=2 << 20,
    )
    a, b = stage[:4], stage[4:]
    a = [a[0]] + [ring_z(a[d], d) for d in range(1, 4)]
    b = [b[0]] + [ring_x(b[d], d) for d in range(1, 4)]
    stage = call(
        last_kernel,
        (1,),
        [pos] + [(whole(quarter), v) for v in a + b],
        [out((PIECE, 256), F32)] * 4,
        moved=1 << 19,
    )
    stage = [stage[0]] + [ring_y(stage[d], d) for d in range(1, 4)]
    (weight_grad,) = call(
        place_kernel,
        (1,),
        [pos] + [(whole((PIECE, 256)), v) for v in stage],
        [out((width // 64, 2, 512), F32)],
        moved=1 << 18,
    )

    (terms,) = call(
        pair_input_kernel,
        (4,),
        [pos]
        + [(small, c) for c in mixed_pair]
        + [(full, base), (column(-1, HEAD), w_key), (column(-1, HEAD), value_weight)],
        [out((rows, width), F32)],
        [pltpu.VMEM((rows, width), F32)],
        flops=2 * rows * width * 1024,
        moved=2 * width * 1024,
    )
    low, high = terms[:, : width // 2], terms[:, width // 2 :]
    kept = jnp.where(core == 0, low, high)
    given = jnp.where(core == 0, high, low).astype(BF)
    input_grad = (kept + other_core(given).astype(F32)).astype(BF)
    return input_grad, weight_grad


def solution(mesh):
    placed = (
        P("seq", None),
        P("seq", None),
        P(None, "mp"),
        P(None, "mp"),
        P(None, "mp"),
        P("mp", None),
    )
    return jax.shard_map(
        on_device,
        mesh=mesh,
        in_specs=placed,
        out_specs=(P("seq", "mp"), P("seq", None, "mp")),
        check_vma=False,
    )
```

```python
import math

import jax
import jax.numpy as jnp
from jax import lax
from jax.experimental import pallas as pl
from jax.experimental.pallas import tpu as pltpu
from jax.sharding import PartitionSpec as P

BF = jnp.bfloat16
F32 = jnp.float32
HEAD = 128
SCALE = 168.0 ** (-0.5)
SCALE2 = SCALE * math.log2(math.e)
PIECE = 42


NT = (((1,), (1,)), ((), ()))
TN = (((0,), (0,)), ((), ()))
NN = (((1,), (0,)), ((), ()))


def mm(a, b, dims=NN):
    return lax.dot_general(a, b, dims, preferred_element_type=F32)


def ring_y(x, d):
    return lax.ppermute(x, "seq", [(i, i // 4 * 4 + (i + d) % 4) for i in range(64)])


def ring_z(x, d):
    return lax.ppermute(
        x, "seq", [(i, i // 16 * 16 + (i // 4 + d) % 4 * 4 + i % 4) for i in range(64)]
    )


def ring_x(x, d):
    return lax.ppermute(x, "seq", [(i, (i // 16 + d) % 4 * 16 + i % 16) for i in range(64)])


def lines_on(x, d):
    return lax.ppermute(x, "seq", [(i, i + 4 * d) for i in range(64) if 0 <= i + 4 * d < 64])


def exchange(ring, chunks):
    got = {d: ring(chunks[d], d) for d in (1, 3, 2)}
    return [chunks[0], got[1], got[2], got[3]]


def other_core(x):
    return lax.ppermute(x, "mp", [(0, 1), (1, 0)])


def call(kernel, grid, ins, outs, scratch=(), flops=0, moved=0, limit=20):
    specs_in, values = zip(*ins[1:])
    specs_out, shapes = zip(*outs)
    return pl.pallas_call(
        kernel,
        grid_spec=pltpu.PrefetchScalarGridSpec(
            num_scalar_prefetch=1,
            grid=grid,
            in_specs=list(specs_in),
            out_specs=list(specs_out),
            scratch_shapes=list(scratch),
        ),
        out_shape=list(shapes),
        compiler_params=pltpu.CompilerParams(
            dimension_semantics=("arbitrary",) * len(grid), vmem_limit_bytes=limit << 20
        ),
        cost_estimate=pl.CostEstimate(flops=flops, bytes_accessed=moved, transcendentals=0),
    )(ins[0], *values)


def flat_call(kernel, ins, outs, scratch=(), flops=0, moved=0, limit=20):
    specs_in, values = zip(*ins[1:])
    _, shapes = zip(*outs)
    return pl.pallas_call(
        kernel,
        in_specs=[pl.BlockSpec(memory_space=pltpu.SMEM)] + list(specs_in),
        out_specs=[pl.BlockSpec(memory_space=pltpu.VMEM)] * len(shapes),
        scratch_shapes=list(scratch),
        out_shape=list(shapes),
        compiler_params=pltpu.CompilerParams(vmem_limit_bytes=limit << 20),
        cost_estimate=pl.CostEstimate(flops=flops, bytes_accessed=moved, transcendentals=0),
    )(ins[0], *values)


def whole(shape):
    return pl.BlockSpec(shape, lambda *_: (0,) * len(shape))


def hbm():
    return pl.BlockSpec(memory_space=pl.ANY)


def far_memory():
    return pl.BlockSpec(memory_space=pltpu.HBM)


def vmem():
    return pl.BlockSpec(memory_space=pltpu.VMEM)


def out(shape, dtype):
    return whole(shape), jax.ShapeDtypeStruct(shape, dtype)


def load_inputs(tok, tan, both, sem):
    rows = tok.shape[0]
    return [
        pltpu.make_async_copy(tok, both.at[pl.ds(0, rows)], sem.at[0]),
        pltpu.make_async_copy(tan, both.at[pl.ds(rows, rows)], sem.at[1]),
    ]


def key_value_kernel(pos, tok, tan, wk, wv, *refs):
    outs, (both, w, sem) = refs[:4], refs[4:]
    rows = tok.shape[0]
    copies = load_inputs(tok, tan, both, sem)
    for d in range(4):
        cols = pl.ds(pl.multiple_of(lax.rem(pos[2] + d, 4) * HEAD, HEAD), HEAD)
        for j, src in enumerate((wk, wv)):
            copies.append(
                pltpu.make_async_copy(
                    src.at[:, cols], w.at[d, :, pl.ds(j * HEAD, HEAD)], sem.at[2 + 2 * d + j]
                )
            )
    for c in copies[:6]:
        c.start()
    copies[0].wait()
    copies[1].wait()
    for d in range(4):
        copies[2 + 2 * d].wait()
        copies[3 + 2 * d].wait()
        for c in copies[6 + 2 * d : 8 + 2 * d]:
            c.start()
        res = mm(both[...], w[d]).astype(BF)
        outs[d][0] = res[:rows, :HEAD]
        outs[d][1] = res[rows:, :HEAD]
        outs[d][2] = res[:rows, HEAD:]
        outs[d][3] = res[rows:, HEAD:]


def query_kernel(pos, tok, tan, w, *refs):
    outs, both = refs[:4], refs[4]
    rows = tok.shape[0]
    both[:rows] = tok[...]
    both[rows:] = tan[...]
    for d in range(4):
        cols = pl.ds(pl.multiple_of(lax.rem(pos[2] + d, 4) * 256, 256), 256)
        res = mm(both[...], w[:, cols]).astype(BF)
        outs[d][0] = res[:rows]
        outs[d][1] = res[rows:]


def join_kernel(pos, a, b, c, e, res):
    res[0] = a[...]
    res[1] = b[...]
    res[2] = c[...]
    res[3] = e[...]


def two_heads(block):
    return jnp.concatenate([block[:, :HEAD], block[:, HEAD:]], axis=0)


def forward_kernel(pos, *refs):
    lines = refs[:3]
    q_refs = refs[3:7]
    o0, o1, o2, o3, k_all, v_all, q_all, p_all, kkd, vvd, qbuf, sems = refs[-12:]
    outs = (o0, o1, o2, o3)
    b = pl.program_id(0)
    y = pos[2]

    @pl.when(b == 0)
    def _():
        copies = []
        for line in range(3):
            for d in range(4):
                row = pl.multiple_of((lax.rem(y + 4 - d, 4) + 4 * line) * HEAD, HEAD)
                src = lines[line].at[d]
                for part in range(4):
                    dst = kkd if part < 2 else vvd
                    copies.append(
                        pltpu.make_async_copy(
                            src.at[part],
                            dst.at[pl.ds(row, HEAD), pl.ds(part % 2 * HEAD, HEAD)],
                            sems.at[line * 16 + d * 4 + part],
                        )
                    )
        for d in range(4):
            copies.append(
                pltpu.make_async_copy(
                    q_refs[d], qbuf.at[lax.rem(y + 4 - d, 4)], sems.at[48 + d]
                )
            )
        for c in copies:
            c.start()
        for c in copies:
            c.wait()
        k_all[...] = kkd[:, :HEAD]
        v_all[...] = vvd[:, :HEAD]

    rows = pl.ds(pl.multiple_of(b * HEAD, HEAD), 9 * HEAD)
    q = two_heads(qbuf[b, 0])
    qd = two_heads(qbuf[b, 1])
    q_all[0] = q
    keys = kkd[rows, :]
    s = mm(keys[:, :HEAD], q, NT)
    u = lax.broadcasted_iota(jnp.int32, s.shape, 0)
    t = lax.rem(lax.broadcasted_iota(jnp.int32, (1, s.shape[1]), 1), HEAD)
    first = 1024 - b * HEAD - 512 * (4 * pos[0] + pos[1])
    allowed = (u >= jnp.maximum(t + 1, first)) & (u <= t + 1024)
    s = jnp.where(allowed, s, -1e30)
    e = jnp.exp2((s - jnp.max(s, axis=0, keepdims=True)) * SCALE2)
    inv = 1.0 / jnp.sum(e, axis=0, keepdims=True)
    sd = mm(keys, jnp.concatenate([qd, q], axis=1), NT)
    mean = jnp.sum(e * sd, axis=0, keepdims=True) * inv
    p_b = (e * inv).astype(BF)
    pd_b = (e * ((sd - mean) * (inv * SCALE))).astype(BF)
    p_all[0] = p_b
    values = vvd[rows, :]
    mixed = mm(values[:, :HEAD], pd_b, TN) + mm(values[:, HEAD:], p_b, TN)
    mixed = jnp.concatenate([mixed[:, :HEAD].T, mixed[:, HEAD:].T], axis=1).astype(BF)
    target = lax.rem(b + 4 - y, 4)
    for d in range(4):

        @pl.when(target == d)
        def _():
            outs[d][...] = mixed


def place_heads(pos, chunks, buf, size):
    for d, c in enumerate(chunks):
        head = lax.rem(pos[2] + 4 - d, 4)
        buf[:, pl.ds(pl.multiple_of(head * size, size), size)] = c


def out_kernel(pos, o0, o1, o2, o3, w, total, sent, buf):
    place_heads(pos, (o0[...], o1[...], o2[...], o3[...]), buf, 256)
    full = mm(buf[...], w[...])
    total[...] = full
    sent[...] = full.astype(BF)


def gradient_kernel(pos, total, other, w, g0, g1, g2, g3, buf):
    ct = (total[...] + other[...].astype(F32)).astype(BF)
    buf[...] = mm(ct, w[...], NT).astype(BF)
    for d, ref in enumerate((g0, g1, g2, g3)):
        head = lax.rem(pos[2] + d, 4)
        ref[...] = buf[:, pl.ds(pl.multiple_of(head * 256, 256), 256)]


def backward_kernel(pos, g0, g1, g2, g3, k_all, v_all, q_all, p_all, *refs):
    q0, q1, q2, q3, own, near, far, dk, dv = refs
    b = pl.program_id(0)
    y = pos[2]
    source = lax.rem(y + 4 - b, 4)
    target = lax.rem(b + 4 - y, 4)

    @pl.when(b == 0)
    def _():
        dk[...] = jnp.zeros_like(dk)
        dv[...] = jnp.zeros_like(dv)

    g = jnp.where(
        source < 2,
        jnp.where(source == 0, g0[...], g1[...]),
        jnp.where(source == 2, g2[...], g3[...]),
    )
    g = two_heads(g)
    rows = pl.ds(pl.multiple_of(b * HEAD, HEAD), 9 * HEAD)
    keys = k_all[rows, :]
    p_b = p_all[0]
    q = q_all[0]
    dp = mm(v_all[rows, :], g, NT)
    p = p_b.astype(F32)
    ds = (p * (dp - jnp.sum(p * dp, axis=0, keepdims=True))).astype(BF)
    dq = mm(keys, ds, TN) * SCALE
    dq = jnp.concatenate([dq[:, :HEAD].T, dq[:, HEAD:].T], axis=1).astype(BF)
    for d, ref in enumerate((q0, q1, q2, q3)):

        @pl.when(target == d)
        def _():
            ref[...] = dq

    dk[rows, :] += mm(ds, q)
    dv[rows, :] += mm(p_b, g)

    @pl.when(b == 3)
    def _():
        far[:, :HEAD] = (dk[:512, :] * SCALE).astype(BF)
        far[:, HEAD:] = dv[:512, :].astype(BF)
        near[:, :HEAD] = (dk[512:1024, :] * SCALE).astype(BF)
        near[:, HEAD:] = dv[512:1024, :].astype(BF)
        own[:, :HEAD] = dk[1024:, :] * SCALE
        own[:, HEAD:] = dv[1024:, :]


def pair_kernel(pos, own, near, far, *outs):
    y = pos[2]
    for d in range(4):
        rows = pl.ds(pl.multiple_of(lax.rem(y + d, 4) * HEAD, HEAD), HEAD)
        outs[d][...] = (
            own[rows, :] + near[rows, :].astype(F32) + far[rows, :].astype(F32)
        ).astype(BF)


def query_input_kernel(pos, q0, q1, q2, q3, w, _, total, buf):
    place_heads(pos, (q0[...], q1[...], q2[...], q3[...]), buf, 256)
    total[...] = mm(buf[...], w[...], NT)


def pair_input_kernel(pos, c0, c1, c2, c3, base, wk, wv, total, kbuf, vbuf):
    chunks = (c0, c1, c2, c3)
    place_heads(pos, [c[:, :HEAD] for c in chunks], kbuf, HEAD)
    place_heads(pos, [c[:, HEAD:] for c in chunks], vbuf, HEAD)
    total[...] = base[...] + (mm(kbuf[...], wk[...], NT) + mm(vbuf[...], wv[...], NT))


def weight_kernel(pos, *refs):
    mine, r1, r2, r3, p1, p2, p3, c0, c1, c2, c3 = refs[:11]
    outs = refs[11:15]
    line, sems = refs[15:]
    core = pos[3]
    half = r1.shape[0]
    copies = [pltpu.make_async_copy(mine, line.at[:, pl.ds(0, HEAD)], sems.at[0])]
    for d, (r, p) in enumerate(((r1, p1), (r2, p2), (r3, p3)), 1):
        for j, (src, where) in enumerate(((r, core), (p, 1 - core))):
            rows = pl.ds(pl.multiple_of(where * half, half), half)
            copies.append(
                pltpu.make_async_copy(
                    src, line.at[rows, pl.ds(d * HEAD, HEAD)], sems.at[2 * d - 1 + j]
                )
            )
    for c in copies:
        c.start()
    for c in copies:
        c.wait()
    pair = jnp.concatenate([c0[...], c3[...], c2[...], c1[...]], axis=0)
    size = 16 * PIECE
    for d in range(4):
        x = lax.rem(pos[0] + d, 4)
        block = line[pl.ds(pl.multiple_of(x * size, size), size), :]
        outs[d][...] = mm(block, pair).astype(BF)


def add_up(ins, rows):
    total = ins[0][rows, :].astype(F32)
    for r in ins[1:]:
        total += r[rows, :].astype(F32)
    return total


def middle_kernel(pos, *refs):
    ins, outs, total = refs[:4], refs[4:8], refs[8]
    size = 4 * PIECE
    total[...] = add_up(ins, slice(None))
    for d in range(4):
        rows = pl.ds(pl.multiple_of(lax.rem(pos[1] + d, 4) * size, 8), size)
        outs[d][...] = total[rows, :].astype(BF)


def last_kernel(pos, *refs):
    ins, outs = refs[:4], refs[4:]
    total = add_up(ins, slice(None))
    parts = [total[i * PIECE : (i + 1) * PIECE] for i in range(4)]
    for d in range(4):
        at = lax.rem(pos[2] + d, 4)
        outs[d][...] = jnp.where(
            at < 2,
            jnp.where(at == 0, parts[0], parts[1]),
            jnp.where(at == 2, parts[2], parts[3]),
        )


def place_kernel(pos, c0, c1, c2, c3, res):
    for d, c in enumerate((c0, c1, c2, c3)):
        head = pl.multiple_of(lax.rem(pos[2] + 4 - d, 4) * HEAD, HEAD)
        for j in range(2):
            res[:, j, pl.ds(head, HEAD)] = c[: res.shape[0], j * HEAD : (j + 1) * HEAD]


def on_device(tokens, tangent, w_query, w_key, value_weight, w_out):
    rows, width = tokens.shape
    seq = lax.axis_index("seq")
    core = lax.axis_index("mp")
    pos = jnp.stack([seq // 16, seq // 4 % 4, seq % 4, core]).astype(jnp.int32)
    piece_out = [out((4, rows, HEAD), BF)] * 4
    tok_in = (far_memory(), tokens)
    tan_in = (far_memory(), tangent)
    kv = flat_call(
        key_value_kernel,
        [pos, tok_in, tan_in, (far_memory(), w_key), (far_memory(), value_weight)],
        piece_out,
        [
            pltpu.VMEM((2 * rows, width), BF),
            pltpu.VMEM((4, width, 256), BF),
            pltpu.SemaphoreType.DMA((10,)),
        ],
        flops=2 * 256 * width * 1024,
        moved=2 * width * 1024,
        limit=62,
    )
    (line,) = flat_call(
        join_kernel,
        [pos] + [(vmem(), c) for c in exchange(ring_y, kv)],
        [out((4, 4, rows, HEAD), BF)],
        moved=1 << 20,
    )
    lines = [lines_on(line, 2), lines_on(line, 1), line]
    q = flat_call(
        query_kernel,
        [pos, (vmem(), tokens), (vmem(), tangent), (vmem(), w_query)],
        [out((2, rows, 256), BF)] * 4,
        [pltpu.VMEM((2 * rows, width), BF)],
        flops=2 * 256 * width * 1024,
        moved=2 * width * 1024,
    )
    late_tokens, _ = lax.optimization_barrier((tokens, q[0]))
    q = exchange(ring_y, q)
    columns = late_tokens.T
    half = lax.dynamic_slice_in_dim(columns, core * (width // 2), width // 2, 0)
    halves = exchange(ring_y, [half] * 4)[1:]
    partner_halves = [other_core(h) for h in halves]

    attended = call(
        forward_kernel,
        (4,),
        [pos] + [(hbm(), a) for a in lines + q],
        [out((rows, 256), BF)] * 4
        + [
            out((1536, HEAD), BF),
            out((1536, HEAD), BF),
            (pl.BlockSpec((1, 256, HEAD), lambda i, p: (i, 0, 0)), jax.ShapeDtypeStruct((4, 256, HEAD), BF)),
            (pl.BlockSpec((1, 1152, 256), lambda i, p: (i, 0, 0)), jax.ShapeDtypeStruct((4, 1152, 256), BF)),
        ],
        [
            pltpu.VMEM((1536, 256), BF),
            pltpu.VMEM((1536, 256), BF),
            pltpu.VMEM((4, 2, rows, 256), BF),
            pltpu.SemaphoreType.DMA((52,)),
        ],
        flops=2 * 4 * 1152 * 256 * 128 * 5,
        moved=8 << 20,
    )
    o, (k_all, v_all, q_all, p_all) = attended[:4], attended[4:]
    o = exchange(ring_y, o)
    small = whole((rows, 256))
    wide = pltpu.VMEM((rows, 1024), BF)
    total, sent = flat_call(
        out_kernel,
        [pos] + [(vmem(), a) for a in o] + [(vmem(), w_out)],
        [out((rows, width), F32), out((rows, width), BF)],
        [wide],
        flops=2 * rows * width * 1024,
        moved=2 * width * 1024,
    )
    other = other_core(sent)
    g = flat_call(
        gradient_kernel,
        [pos, (vmem(), total), (vmem(), other), (vmem(), w_out)],
        [out((rows, 256), BF)] * 4,
        [wide],
        flops=2 * rows * width * 1024,
        moved=2 * width * 1024,
    )
    g = exchange(ring_y, g)
    back = call(
        backward_kernel,
        (4,),
        [pos]
        + [(small, a) for a in g]
        + [
            (whole((1536, HEAD)), k_all),
            (whole((1536, HEAD)), v_all),
            (pl.BlockSpec((1, 256, HEAD), lambda i, p: (i, 0, 0)), q_all),
            (pl.BlockSpec((1, 1152, 256), lambda i, p: (i, 0, 0)), p_all),
        ],
        [out((rows, 256), BF)] * 4 + [out((512, 256), F32), out((512, 256), BF), out((512, 256), BF)],
        [pltpu.VMEM((1536, HEAD), F32), pltpu.VMEM((1536, HEAD), F32)],
        flops=2 * 4 * 1152 * 256 * 128 * 4,
        moved=6 << 20,
    )
    dq, (own, to_near, to_far) = back[:4], back[4:]
    from_far = lines_on(to_far, -2)
    from_near = lines_on(to_near, -1)
    dq = exchange(ring_y, dq)
    pair = call(
        pair_kernel,
        (1,),
        [pos] + [(whole((512, 256)), a) for a in (own, from_near, from_far)],
        [out((rows, 256), BF)] * 4,
        moved=1 << 20,
    )
    mixed_pair = exchange(ring_y, pair)

    part = (16 * PIECE, 256)
    stage = call(
        weight_kernel,
        (1,),
        [pos] + [(hbm(), a) for a in [columns] + halves + partner_halves] + [(small, a) for a in pair],
        [out(part, BF)] * 4,
        [pltpu.VMEM((64 * PIECE, 512), BF), pltpu.SemaphoreType.DMA((7,))],
        flops=2 * 3072 * 512 * 256,
        moved=5 << 20,
    )
    first = stage[0]
    stage = exchange(ring_x, stage)
    stage = flat_call(
        middle_kernel,
        [pos] + [(vmem(), v) for v in stage],
        [out((4 * PIECE, 256), BF)] * 4,
        [pltpu.VMEM((16 * PIECE, 256), F32)],
        moved=2 << 20,
    )
    stage = exchange(ring_z, stage)
    stage = flat_call(
        last_kernel,
        [pos] + [(vmem(), v) for v in stage],
        [out((PIECE, 256), F32)] * 4,
        moved=1 << 19,
    )
    stage = exchange(ring_y, stage)
    (weight_grad,) = call(
        place_kernel,
        (1,),
        [pos] + [(whole((PIECE, 256)), v) for v in stage],
        [out((width // 64, 2, 512), F32)],
        moved=1 << 18,
    )

    (base,) = flat_call(
        query_input_kernel,
        [pos] + [(vmem(), a) for a in dq] + [(vmem(), w_query), (hbm(), first)],
        [out((rows, width), F32)],
        [wide],
        flops=2 * rows * width * 1024,
        moved=2 * width * 1024,
    )
    narrow = pltpu.VMEM((rows, 512), BF)
    (terms,) = flat_call(
        pair_input_kernel,
        [pos]
        + [(vmem(), c) for c in mixed_pair]
        + [(vmem(), base), (vmem(), w_key), (vmem(), value_weight)],
        [out((rows, width), F32)],
        [narrow, narrow],
        flops=2 * rows * width * 1024,
        moved=2 * width * 1024,
    )
    low, high = terms[:, : width // 2], terms[:, width // 2 :]
    kept = jnp.where(core == 0, low, high)
    given = jnp.where(core == 0, high, low).astype(BF)
    input_grad = (kept + other_core(given).astype(F32)).astype(BF)
    return input_grad, weight_grad


def solution(mesh):
    placed = (
        P("seq", None),
        P("seq", None),
        P(None, "mp"),
        P(None, "mp"),
        P(None, "mp"),
        P("mp", None),
    )
    return jax.shard_map(
        on_device,
        mesh=mesh,
        in_specs=placed,
        out_specs=(P("seq", "mp"), P("seq", None, "mp")),
        check_vma=False,
    )
```

```python
import math

import jax
import jax.numpy as jnp
from jax import lax
from jax.experimental import pallas as pl
from jax.experimental.pallas import tpu as pltpu
from jax.sharding import PartitionSpec as P

BF = jnp.bfloat16
F32 = jnp.float32
HEAD = 128
SCALE = 168.0 ** (-0.5)
SCALE2 = SCALE * math.log2(math.e)
PIECE = 42


NT = (((1,), (1,)), ((), ()))
TN = (((0,), (0,)), ((), ()))
NN = (((1,), (0,)), ((), ()))


def mm(a, b, dims=NN):
    return lax.dot_general(a, b, dims, preferred_element_type=F32)


def ring_y(x, d):
    return lax.ppermute(x, "seq", [(i, i // 4 * 4 + (i + d) % 4) for i in range(64)])


def ring_z(x, d):
    return lax.ppermute(
        x, "seq", [(i, i // 16 * 16 + (i // 4 + d) % 4 * 4 + i % 4) for i in range(64)]
    )


def ring_x(x, d):
    return lax.ppermute(x, "seq", [(i, (i // 16 + d) % 4 * 16 + i % 16) for i in range(64)])


def lines_on(x, d):
    return lax.ppermute(x, "seq", [(i, i + 4 * d) for i in range(64) if 0 <= i + 4 * d < 64])


def exchange(ring, chunks):
    got = {d: ring(chunks[d], d) for d in (1, 3, 2)}
    return [chunks[0], got[1], got[2], got[3]]


def far_one(x):
    return lax.ppermute(
        x, "seq", [(i, i // 16 * 16 + (i // 4 + 3) % 4 * 4 + i % 4) for i in range(64)]
    )


def far_two(x):
    route = []
    for i in range(64):
        source = i // 16 * 16 + (i // 4 + 1) % 4 * 4 + i % 4
        if source + 8 < 64:
            route.append((i, source + 8))
    return lax.ppermute(x, "seq", route)


def other_core(x):
    return lax.ppermute(x, "mp", [(0, 1), (1, 0)])


def call(kernel, grid, ins, outs, scratch=(), flops=0, moved=0, limit=20):
    specs_in, values = zip(*ins[1:])
    specs_out, shapes = zip(*outs)
    return pl.pallas_call(
        kernel,
        grid_spec=pltpu.PrefetchScalarGridSpec(
            num_scalar_prefetch=1,
            grid=grid,
            in_specs=list(specs_in),
            out_specs=list(specs_out),
            scratch_shapes=list(scratch),
        ),
        out_shape=list(shapes),
        compiler_params=pltpu.CompilerParams(
            dimension_semantics=("arbitrary",) * len(grid), vmem_limit_bytes=limit << 20
        ),
        cost_estimate=pl.CostEstimate(flops=flops, bytes_accessed=moved, transcendentals=0),
    )(ins[0], *values)


def flat_call(kernel, ins, outs, scratch=(), flops=0, moved=0, limit=20):
    specs_in, values = zip(*ins[1:])
    _, shapes = zip(*outs)
    return pl.pallas_call(
        kernel,
        in_specs=[pl.BlockSpec(memory_space=pltpu.SMEM)] + list(specs_in),
        out_specs=[pl.BlockSpec(memory_space=pltpu.VMEM)] * len(shapes),
        scratch_shapes=list(scratch),
        out_shape=list(shapes),
        compiler_params=pltpu.CompilerParams(vmem_limit_bytes=limit << 20),
        cost_estimate=pl.CostEstimate(flops=flops, bytes_accessed=moved, transcendentals=0),
    )(ins[0], *values)


def whole(shape):
    return pl.BlockSpec(shape, lambda *_: (0,) * len(shape))


def hbm():
    return pl.BlockSpec(memory_space=pl.ANY)


def far_memory():
    return pl.BlockSpec(memory_space=pltpu.HBM)


def vmem():
    return pl.BlockSpec(memory_space=pltpu.VMEM)


def out(shape, dtype):
    return whole(shape), jax.ShapeDtypeStruct(shape, dtype)


CUTS = (0, 640, 1280, 1920, 2688)


def key_value_kernel(pos, tok, tan, wk, wv, *refs):
    outs, (both, w, acc, flat, sem) = refs[:4], refs[4:]
    rows = tok.shape[0]
    half = wk.shape[1]
    copies = [
        pltpu.make_async_copy(tok, both.at[pl.ds(0, rows)], sem.at[0]),
        pltpu.make_async_copy(tan, both.at[pl.ds(rows, rows)], sem.at[1]),
    ]
    for j in range(4):
        part = pl.ds(CUTS[j], CUTS[j + 1] - CUTS[j])
        for i, src in enumerate((wk, wv)):
            copies.append(
                pltpu.make_async_copy(
                    src.at[part], w.at[part, pl.ds(i * half, half)], sem.at[2 + 2 * j + i]
                )
            )
    for c in copies[:6]:
        c.start()
    copies[0].wait()
    copies[1].wait()
    for j in range(4):
        copies[2 + 2 * j].wait()
        copies[3 + 2 * j].wait()
        for c in copies[6 + 2 * j : 8 + 2 * j]:
            c.start()
        part = slice(CUTS[j], CUTS[j + 1])
        res = mm(both[:, part], w[part, :])
        if j == 0:
            acc[...] = res
        elif j < 3:
            acc[...] += res
        else:
            flat[...] = (acc[...] + res).astype(BF)
    for d in range(4):
        head = lax.rem(pos[2] + d, 4) * HEAD
        k = flat[:, pl.ds(pl.multiple_of(head, HEAD), HEAD)]
        v = flat[:, pl.ds(pl.multiple_of(head + half, HEAD), HEAD)]
        outs[d][0] = k[:rows]
        outs[d][1] = k[rows:]
        outs[d][2] = v[:rows]
        outs[d][3] = v[rows:]


def query_kernel(pos, tok, tan, w, *refs):
    outs, both = refs[:4], refs[4]
    rows = tok.shape[0]
    both[:rows] = tok[...]
    both[rows:] = tan[...]
    for d in range(4):
        cols = pl.ds(pl.multiple_of(lax.rem(pos[2] + d, 4) * 256, 256), 256)
        res = mm(both[...], w[:, cols]).astype(BF)
        outs[d][0] = res[:rows]
        outs[d][1] = res[rows:]


def join_kernel(pos, a, b, c, e, line, low, high):
    for d, ref in enumerate((a, b, c, e)):
        block = lax.rem(pos[2] + 4 - d, 4)
        rows = pl.ds(pl.multiple_of(block * HEAD, HEAD), HEAD)
        for part in range(4):
            line[rows, part * HEAD : (part + 1) * HEAD] = ref[part]
    low[...] = line[:256]
    high[...] = line[256:]


def load_kernel(pos, src, dst, sem):
    copy = pltpu.make_async_copy(src, dst, sem)
    copy.start()
    copy.wait()


def two_heads(block):
    return jnp.concatenate([block[:, :HEAD], block[:, HEAD:]], axis=0)


def window_of(refs, b, cols):
    low, high, near, own = refs
    parts = []
    if b < 2:
        parts.append(low[b * HEAD :, cols])
        parts.append(high[:, cols])
    else:
        parts.append(high[(b - 2) * HEAD :, cols])
    parts += [near[:, cols], own[: (b + 1) * HEAD, cols]]
    return jnp.concatenate(parts, axis=0)


def forward_kernel(pos, low, high, near, own, q0, q1, q2, q3, *refs):
    o0, o1, o2, o3, q_all, p_all, qbuf, obuf = refs
    lines = (low, high, near, own)
    line = 4 * pos[0] + pos[1]
    far_bias = jnp.where(line < 2, -1e30, 0.0).astype(F32)
    near_bias = jnp.where(line < 1, -1e30, 0.0).astype(F32)
    for d, q in enumerate((q0, q1, q2, q3)):
        qbuf[lax.rem(pos[2] + 4 - d, 4)] = q[...]
    u = lax.broadcasted_iota(jnp.int32, (HEAD, 256), 0)
    t = lax.rem(lax.broadcasted_iota(jnp.int32, (HEAD, 256), 1), HEAD)
    for b in range(4):
        q = two_heads(qbuf[b, 0])
        qd = two_heads(qbuf[b, 1])
        q_all[b] = q
        keys = window_of(lines, b, slice(0, 256))
        values = window_of(lines, b, slice(256, 512))
        s = mm(keys[:, :HEAD], q, NT)
        split = (4 - b) * HEAD
        parts = [jnp.where(u > t, s[:HEAD] + far_bias, -1e30)]
        if b < 3:
            parts.append(s[HEAD:split] + far_bias)
        parts.append(s[split : split + 512] + near_bias)
        if b > 0:
            parts.append(s[split + 512 : 8 * HEAD])
        parts.append(jnp.where(u <= t, s[8 * HEAD :], -1e30))
        s = jnp.concatenate(parts, axis=0)
        e = jnp.exp2((s - jnp.max(s, axis=0, keepdims=True)) * SCALE2)
        inv = 1.0 / jnp.sum(e, axis=0, keepdims=True)
        sd = mm(keys, jnp.concatenate([qd, q], axis=1), NT)
        mean = jnp.sum(e * sd, axis=0, keepdims=True) * inv
        p_b = (e * inv).astype(BF)
        pd_b = (e * ((sd - mean) * (inv * SCALE))).astype(BF)
        p_all[b] = p_b
        mixed = mm(values[:, :HEAD], pd_b, TN) + mm(values[:, HEAD:], p_b, TN)
        obuf[b, :, :HEAD] = mixed[:, :HEAD].T.astype(BF)
        obuf[b, :, HEAD:] = mixed[:, HEAD:].T.astype(BF)
    for d, o in enumerate((o0, o1, o2, o3)):
        o[...] = obuf[lax.rem(pos[2] + d, 4)]


def place_heads(pos, chunks, buf, size):
    for d, c in enumerate(chunks):
        head = lax.rem(pos[2] + 4 - d, 4)
        buf[:, pl.ds(pl.multiple_of(head * size, size), size)] = c


def out_kernel(pos, o0, o1, o2, o3, w, total, sent, buf):
    place_heads(pos, (o0[...], o1[...], o2[...], o3[...]), buf, 256)
    full = mm(buf[...], w[...])
    total[...] = full
    sent[...] = full.astype(BF)


def gradient_kernel(pos, total, other, w, g0, g1, g2, g3, buf):
    ct = (total[...] + other[...].astype(F32)).astype(BF)
    buf[...] = mm(ct, w[...], NT).astype(BF)
    for d, ref in enumerate((g0, g1, g2, g3)):
        head = lax.rem(pos[2] + d, 4)
        ref[...] = buf[:, pl.ds(pl.multiple_of(head * 256, 256), 256)]


def backward_kernel(pos, g0, g1, g2, g3, low, high, near_kv, own_kv, q_all, p_all, *refs):
    q0, q1, q2, q3, own, near, far, dk, dv, gbuf, dqbuf = refs
    lines = (low, high, near_kv, own_kv)
    for d, g in enumerate((g0, g1, g2, g3)):
        gbuf[lax.rem(pos[2] + 4 - d, 4)] = g[...]
    for b in range(4):
        g = two_heads(gbuf[b])
        keys = window_of(lines, b, slice(0, HEAD))
        values = window_of(lines, b, slice(256, 384))
        p_b = p_all[b]
        dp = mm(values, g, NT)
        p = p_b.astype(F32)
        ds = (p * (dp - jnp.sum(p * dp, axis=0, keepdims=True))).astype(BF)
        dq = mm(keys, ds, TN) * SCALE
        dqbuf[b, :, :HEAD] = dq[:, :HEAD].T.astype(BF)
        dqbuf[b, :, HEAD:] = dq[:, HEAD:].T.astype(BF)
        dk_part = mm(ds, q_all[b])
        dv_part = mm(p_b, g)
        rows = slice(b * HEAD, b * HEAD + 9 * HEAD)
        if b == 0:
            dk[rows] = dk_part
            dv[rows] = dv_part
        else:
            fresh = slice(b * HEAD + 8 * HEAD, b * HEAD + 9 * HEAD)
            rows = slice(b * HEAD, b * HEAD + 8 * HEAD)
            dk[rows] += dk_part[: 8 * HEAD]
            dv[rows] += dv_part[: 8 * HEAD]
            dk[fresh] = dk_part[8 * HEAD :]
            dv[fresh] = dv_part[8 * HEAD :]
    far[:, :HEAD] = (dk[:512, :] * SCALE).astype(BF)
    far[:, HEAD:] = dv[:512, :].astype(BF)
    near[:, :HEAD] = (dk[512:1024, :] * SCALE).astype(BF)
    near[:, HEAD:] = dv[512:1024, :].astype(BF)
    own[:, :HEAD] = dk[1024:, :] * SCALE
    own[:, HEAD:] = dv[1024:, :]
    for d, q in enumerate((q0, q1, q2, q3)):
        q[...] = dqbuf[lax.rem(pos[2] + d, 4)]


def pair_kernel(pos, own, near, far, *outs):
    y = pos[2]
    for d in range(4):
        rows = pl.ds(pl.multiple_of(lax.rem(y + d, 4) * HEAD, HEAD), HEAD)
        outs[d][...] = (
            own[rows, :] + near[rows, :].astype(F32) + far[rows, :].astype(F32)
        ).astype(BF)


def query_input_kernel(pos, q0, q1, q2, q3, w, _, total, buf):
    place_heads(pos, (q0[...], q1[...], q2[...], q3[...]), buf, 256)
    total[...] = mm(w[...], buf[...], NT)


def pair_input_kernel(pos, c0, c1, c2, c3, base, wk, wv, kept, given, kbuf, vbuf, total):
    chunks = (c0, c1, c2, c3)
    place_heads(pos, [c[:, :HEAD] for c in chunks], kbuf, HEAD)
    place_heads(pos, [c[:, HEAD:] for c in chunks], vbuf, HEAD)
    total[...] = base[...] + (mm(wk[...], kbuf[...], NT) + mm(wv[...], vbuf[...], NT))
    half = kept.shape[0]
    kept[...] = total[pl.ds(pl.multiple_of(pos[3] * half, half), half), :]
    given[...] = total[pl.ds(pl.multiple_of((1 - pos[3]) * half, half), half), :].astype(BF)


def weight_kernel(pos, *refs):
    mine, r1, r2, r3, p1, p2, p3, c0, c1, c2, c3 = refs[:11]
    outs = refs[11:17]
    line, sems = refs[17:]
    core = pos[3]
    half = r1.shape[0]
    copies = [pltpu.make_async_copy(mine, line.at[:, pl.ds(0, HEAD)], sems.at[0])]
    for d, (r, p) in enumerate(((r1, p1), (r2, p2), (r3, p3)), 1):
        for j, (src, where) in enumerate(((r, core), (p, 1 - core))):
            rows = pl.ds(pl.multiple_of(where * half, half), half)
            copies.append(
                pltpu.make_async_copy(
                    src, line.at[rows, pl.ds(d * HEAD, HEAD)], sems.at[2 * d - 1 + j]
                )
            )
    for c in copies:
        c.start()
    for c in copies:
        c.wait()
    pair = jnp.concatenate([c0[...], c3[...], c2[...], c1[...]], axis=0)
    size = 16 * PIECE
    for d in range(4):
        x = lax.rem(pos[0] + d, 4)
        block = line[pl.ds(pl.multiple_of(x * size, size), size), :]
        part = mm(block, pair).astype(BF)
        outs[d][...] = part
        if d == 2:
            outs[4][...] = part[: size // 2]
            outs[5][...] = part[size // 2 :]


def across(stage):
    up = ring_x(stage[4], 1)
    down = ring_x(stage[5], 3)
    one, three = ring_x(stage[1], 1), ring_x(stage[3], 3)
    up, down = ring_x(up, 1), ring_x(down, 3)
    return [stage[0], one, three, up, down]


def add_up(ins, rows):
    total = ins[0][rows, :].astype(F32)
    for r in ins[1:]:
        total += r[rows, :].astype(F32)
    return total


def middle_kernel(pos, mine, one, three, up, down, *refs):
    outs, total = refs[:4], refs[4]
    size = 4 * PIECE
    for i, half in enumerate((up, down)):
        rows = slice(i * half.shape[0], (i + 1) * half.shape[0])
        total[rows, :] = add_up((mine, one, three), rows) + half[...].astype(F32)
    for d in range(4):
        rows = pl.ds(pl.multiple_of(lax.rem(pos[1] + d, 4) * size, 8), size)
        outs[d][...] = total[rows, :].astype(BF)


def last_kernel(pos, *refs):
    ins, outs = refs[:4], refs[4:]
    total = add_up(ins, slice(None))
    parts = [total[i * PIECE : (i + 1) * PIECE] for i in range(4)]
    for d in range(4):
        at = lax.rem(pos[2] + d, 4)
        outs[d][...] = jnp.where(
            at < 2,
            jnp.where(at == 0, parts[0], parts[1]),
            jnp.where(at == 2, parts[2], parts[3]),
        )


def place_kernel(pos, c0, c1, c2, c3, res):
    for d, c in enumerate((c0, c1, c2, c3)):
        head = pl.multiple_of(lax.rem(pos[2] + 4 - d, 4) * HEAD, HEAD)
        for j in range(2):
            res[:, j, pl.ds(head, HEAD)] = c[: res.shape[0], j * HEAD : (j + 1) * HEAD]


def on_device(tokens, tangent, w_query, w_key, value_weight, w_out):
    rows, width = tokens.shape
    seq = lax.axis_index("seq")
    core = lax.axis_index("mp")
    pos = jnp.stack([seq // 16, seq // 4 % 4, seq % 4, core]).astype(jnp.int32)
    piece_out = [out((4, rows, HEAD), BF)] * 4
    tok_in = (far_memory(), tokens)
    tan_in = (far_memory(), tangent)
    kv = flat_call(
        key_value_kernel,
        [pos, tok_in, tan_in, (far_memory(), w_key), (far_memory(), value_weight)],
        piece_out,
        [
            pltpu.VMEM((2 * rows, width), BF),
            pltpu.VMEM((width, 1024), BF),
            pltpu.VMEM((2 * rows, 1024), F32),
            pltpu.VMEM((2 * rows, 1024), BF),
            pltpu.SemaphoreType.DMA((10,)),
        ],
        flops=2 * 256 * width * 1024,
        moved=2 * width * 1024,
        limit=62,
    )
    line, low, high = flat_call(
        join_kernel,
        [pos] + [(vmem(), c) for c in exchange(ring_y, kv)],
        [out((512, 512), BF), out((256, 512), BF), out((256, 512), BF)],
        moved=1 << 20,
    )
    passed = far_one(high)
    near = lines_on(line, 1)
    far_low = lines_on(low, 2)
    far_high = far_two(passed)
    lines = [far_low, far_high, near, line]
    q = flat_call(
        query_kernel,
        [pos, (vmem(), tokens), (vmem(), tangent), (vmem(), w_query)],
        [out((2, rows, 256), BF)] * 4,
        [pltpu.VMEM((2 * rows, width), BF)],
        flops=2 * 256 * width * 1024,
        moved=2 * width * 1024,
    )
    late_tokens, _ = lax.optimization_barrier((tokens, q[0]))
    q = exchange(ring_y, q)
    columns = late_tokens.T
    half = lax.dynamic_slice_in_dim(columns, core * (width // 2), width // 2, 0)
    (w_out,) = flat_call(
        load_kernel,
        [pos, (far_memory(), w_out)],
        [out(w_out.shape, BF)],
        [pltpu.SemaphoreType.DMA],
        moved=2 * w_out.size,
    )
    halves = exchange(ring_y, [half] * 4)[1:]
    partner_halves = [other_core(h) for h in halves]

    attended = flat_call(
        forward_kernel,
        [pos] + [(vmem(), a) for a in lines + q],
        [out((rows, 256), BF)] * 4 + [out((4, 256, HEAD), BF), out((4, 1152, 256), BF)],
        [pltpu.VMEM((4, 2, rows, 256), BF), pltpu.VMEM((4, rows, 256), BF)],
        flops=2 * 4 * 1152 * 256 * 128 * 5,
        moved=8 << 20,
        limit=24,
    )
    o, (q_all, p_all) = attended[:4], attended[4:]
    o = exchange(ring_y, o)
    small = whole((rows, 256))
    wide = pltpu.VMEM((rows, 1024), BF)
    total, sent = flat_call(
        out_kernel,
        [pos] + [(vmem(), a) for a in o] + [(vmem(), w_out)],
        [out((rows, width), F32), out((rows, width), BF)],
        [wide],
        flops=2 * rows * width * 1024,
        moved=2 * width * 1024,
    )
    other = other_core(sent)
    g = flat_call(
        gradient_kernel,
        [pos, (vmem(), total), (vmem(), other), (vmem(), w_out)],
        [out((rows, 256), BF)] * 4,
        [wide],
        flops=2 * rows * width * 1024,
        moved=2 * width * 1024,
    )
    g = exchange(ring_y, g)
    back = flat_call(
        backward_kernel,
        [pos] + [(vmem(), a) for a in g + lines + [q_all, p_all]],
        [out((rows, 256), BF)] * 4 + [out((512, 256), F32), out((512, 256), BF), out((512, 256), BF)],
        [
            pltpu.VMEM((1536, HEAD), F32),
            pltpu.VMEM((1536, HEAD), F32),
            pltpu.VMEM((4, rows, 256), BF),
            pltpu.VMEM((4, rows, 256), BF),
        ],
        flops=2 * 4 * 1152 * 256 * 128 * 4,
        moved=6 << 20,
        limit=24,
    )
    dq, (own, to_near, to_far) = back[:4], back[4:]
    from_far = lines_on(to_far, -2)
    from_near = lines_on(to_near, -1)
    dq = exchange(ring_y, dq)
    pair = call(
        pair_kernel,
        (1,),
        [pos] + [(whole((512, 256)), a) for a in (own, from_near, from_far)],
        [out((rows, 256), BF)] * 4,
        moved=1 << 20,
    )
    mixed_pair = exchange(ring_y, pair)

    part = (16 * PIECE, 256)
    stage = call(
        weight_kernel,
        (1,),
        [pos] + [(hbm(), a) for a in [columns] + halves + partner_halves] + [(small, a) for a in pair],
        [out(part, BF)] * 4 + [out((8 * PIECE, 256), BF)] * 2,
        [pltpu.VMEM((64 * PIECE, 512), BF), pltpu.SemaphoreType.DMA((7,))],
        flops=2 * 3072 * 512 * 256,
        moved=5 << 20,
    )
    first = stage[0]
    stage = across(stage)
    stage = flat_call(
        middle_kernel,
        [pos] + [(vmem(), v) for v in stage],
        [out((4 * PIECE, 256), BF)] * 4,
        [pltpu.VMEM((16 * PIECE, 256), F32)],
        moved=2 << 20,
    )
    stage = exchange(ring_z, stage)
    stage = flat_call(
        last_kernel,
        [pos] + [(vmem(), v) for v in stage],
        [out((PIECE, 256), F32)] * 4,
        moved=1 << 19,
    )
    stage = exchange(ring_y, stage)
    (weight_grad,) = call(
        place_kernel,
        (1,),
        [pos] + [(whole((PIECE, 256)), v) for v in stage],
        [out((width // 64, 2, 512), F32)],
        moved=1 << 18,
    )

    (base,) = flat_call(
        query_input_kernel,
        [pos] + [(vmem(), a) for a in dq] + [(vmem(), w_query), (hbm(), first)],
        [out((width, rows), F32)],
        [wide],
        flops=2 * rows * width * 1024,
        moved=2 * width * 1024,
    )
    narrow = pltpu.VMEM((rows, 512), BF)
    kept, given = flat_call(
        pair_input_kernel,
        [pos]
        + [(vmem(), c) for c in mixed_pair]
        + [(vmem(), base), (vmem(), w_key), (vmem(), value_weight)],
        [out((width // 2, rows), F32), out((width // 2, rows), BF)],
        [narrow, narrow, pltpu.VMEM((width, rows), F32)],
        flops=2 * rows * width * 1024,
        moved=2 * width * 1024,
    )
    theirs = other_core(given)
    input_grad = (kept + theirs.astype(F32)).astype(BF).T
    return input_grad, weight_grad


def solution(mesh):
    placed = (
        P("seq", None),
        P("seq", None),
        P(None, "mp"),
        P(None, "mp"),
        P(None, "mp"),
        P("mp", None),
    )
    return jax.shard_map(
        on_device,
        mesh=mesh,
        in_specs=placed,
        out_specs=(P("seq", "mp"), P("seq", None, "mp")),
        check_vma=False,
    )
```

```python
import math

import jax
import jax.numpy as jnp
from jax import lax
from jax.experimental import pallas as pl
from jax.experimental.pallas import tpu as pltpu
from jax.sharding import PartitionSpec as P

BF = jnp.bfloat16
F32 = jnp.float32
HEAD = 128
SCALE = 168.0 ** (-0.5)
SCALE2 = SCALE * math.log2(math.e)
PIECE = 42


NT = (((1,), (1,)), ((), ()))
TN = (((0,), (0,)), ((), ()))
NN = (((1,), (0,)), ((), ()))


def mm(a, b, dims=NN):
    return lax.dot_general(a, b, dims, preferred_element_type=F32)


def ring_y(x, d):
    return lax.ppermute(x, "seq", [(i, i // 4 * 4 + (i + d) % 4) for i in range(64)])


def ring_z(x, d):
    return lax.ppermute(
        x, "seq", [(i, i // 16 * 16 + (i // 4 + d) % 4 * 4 + i % 4) for i in range(64)]
    )


def ring_x(x, d):
    return lax.ppermute(x, "seq", [(i, (i // 16 + d) % 4 * 16 + i % 16) for i in range(64)])


def lines_on(x, d):
    return lax.ppermute(x, "seq", [(i, (i + 4 * d) % 64) for i in range(64)])


def exchange(ring, chunks):
    got = {d: ring(chunks[d], d) for d in (1, 3, 2)}
    return [chunks[0], got[1], got[2], got[3]]


def far_one(x):
    return lax.ppermute(
        x, "seq", [(i, i // 16 * 16 + (i // 4 + 3) % 4 * 4 + i % 4) for i in range(64)]
    )


def far_two(x):
    route = []
    for i in range(64):
        source = i // 16 * 16 + (i // 4 + 1) % 4 * 4 + i % 4
        route.append((i, (source + 8) % 64))
    return lax.ppermute(x, "seq", route)


def other_core(x):
    return lax.ppermute(x, "mp", [(0, 1), (1, 0)])


def call(kernel, grid, ins, outs, scratch=(), flops=0, moved=0, limit=20):
    specs_in, values = zip(*ins[1:])
    specs_out, shapes = zip(*outs)
    return pl.pallas_call(
        kernel,
        grid_spec=pltpu.PrefetchScalarGridSpec(
            num_scalar_prefetch=1,
            grid=grid,
            in_specs=list(specs_in),
            out_specs=list(specs_out),
            scratch_shapes=list(scratch),
        ),
        out_shape=list(shapes),
        compiler_params=pltpu.CompilerParams(
            dimension_semantics=("arbitrary",) * len(grid), vmem_limit_bytes=limit << 20
        ),
        cost_estimate=pl.CostEstimate(flops=flops, bytes_accessed=moved, transcendentals=0),
    )(ins[0], *values)


def flat_call(kernel, ins, outs, scratch=(), flops=0, moved=0, limit=20):
    specs_in, values = zip(*ins[1:])
    if ins[0] is not None:
        specs_in = (pl.BlockSpec(memory_space=pltpu.SMEM),) + specs_in
        values = (ins[0],) + values
    _, shapes = zip(*outs)
    return pl.pallas_call(
        kernel,
        in_specs=list(specs_in),
        out_specs=[pl.BlockSpec(memory_space=pltpu.VMEM)] * len(shapes),
        scratch_shapes=list(scratch),
        out_shape=list(shapes),
        compiler_params=pltpu.CompilerParams(vmem_limit_bytes=limit << 20),
        cost_estimate=pl.CostEstimate(flops=flops, bytes_accessed=moved, transcendentals=0),
    )(*values)


def whole(shape):
    return pl.BlockSpec(shape, lambda *_: (0,) * len(shape))


def hbm():
    return pl.BlockSpec(memory_space=pl.ANY)


def far_memory():
    return pl.BlockSpec(memory_space=pltpu.HBM)


def vmem():
    return pl.BlockSpec(memory_space=pltpu.VMEM)


def out(shape, dtype):
    return whole(shape), jax.ShapeDtypeStruct(shape, dtype)


CUTS = (0, 512, 1152, 1920, 2688)


def key_value_kernel(tok, tan, wk, wv, *refs):
    y = lax.rem(lax.axis_index("seq"), 4)
    outs, (both, w, acc, flat, sem) = refs[:4], refs[4:]
    rows = tok.shape[0]
    half = wk.shape[1]
    copies = [
        pltpu.make_async_copy(tok, both.at[pl.ds(0, rows)], sem.at[0]),
        pltpu.make_async_copy(tan, both.at[pl.ds(rows, rows)], sem.at[1]),
    ]
    for j in range(4):
        part = pl.ds(CUTS[j], CUTS[j + 1] - CUTS[j])
        for i, src in enumerate((wk, wv)):
            copies.append(
                pltpu.make_async_copy(
                    src.at[part], w.at[part, pl.ds(i * half, half)], sem.at[2 + 2 * j + i]
                )
            )
    for c in copies[:6]:
        c.start()
    copies[0].wait()
    copies[1].wait()
    for j in range(4):
        copies[2 + 2 * j].wait()
        copies[3 + 2 * j].wait()
        for c in copies[6 + 2 * j : 8 + 2 * j]:
            c.start()
        part = slice(CUTS[j], CUTS[j + 1])
        res = mm(both[:, part], w[part, :])
        if j == 0:
            acc[...] = res
        elif j < 3:
            acc[...] += res
        else:
            flat[...] = (acc[...] + res).astype(BF)
    for d in range(4):
        head = lax.rem(y + d, 4) * HEAD
        k = flat[:, pl.ds(pl.multiple_of(head, HEAD), HEAD)]
        v = flat[:, pl.ds(pl.multiple_of(head + half, HEAD), HEAD)]
        outs[d][0] = k[:rows]
        outs[d][1] = k[rows:]
        outs[d][2] = v[:rows]
        outs[d][3] = v[rows:]


def query_kernel(pos, tok, tan, w, *refs):
    outs, both = refs[:4], refs[4]
    rows = tok.shape[0]
    both[:rows] = tok[...]
    both[rows:] = tan[...]
    for d in range(4):
        cols = pl.ds(pl.multiple_of(lax.rem(pos[2] + d, 4) * 256, 256), 256)
        res = mm(both[...], w[:, cols]).astype(BF)
        outs[d][0] = res[:rows]
        outs[d][1] = res[rows:]


def join_kernel(pos, a, b, c, e, line, low, high):
    for d, ref in enumerate((a, b, c, e)):
        block = lax.rem(pos[2] + 4 - d, 4)
        rows = pl.ds(pl.multiple_of(block * HEAD, HEAD), HEAD)
        for part in range(4):
            line[rows, part * HEAD : (part + 1) * HEAD] = ref[part]
    low[...] = line[:256]
    high[...] = line[256:]


def load_kernel(pos, src, dst, sem):
    copy = pltpu.make_async_copy(src, dst, sem)
    copy.start()
    copy.wait()


def two_heads(block):
    return jnp.concatenate([block[:, :HEAD], block[:, HEAD:]], axis=0)


def window_of(refs, b, cols):
    low, high, near, own = refs
    parts = []
    if b < 2:
        parts.append(low[b * HEAD :, cols])
        parts.append(high[:, cols])
    else:
        parts.append(high[(b - 2) * HEAD :, cols])
    parts += [near[:, cols], own[: (b + 1) * HEAD, cols]]
    return jnp.concatenate(parts, axis=0)


def forward_kernel(pos, low, high, near, own, q0, q1, q2, q3, *refs):
    o0, o1, o2, o3, q_all, p_all, qbuf, obuf = refs
    lines = (low, high, near, own)
    line = 4 * pos[0] + pos[1]
    far_bias = jnp.where(line < 2, -1e30, 0.0).astype(F32)
    near_bias = jnp.where(line < 1, -1e30, 0.0).astype(F32)
    for d, q in enumerate((q0, q1, q2, q3)):
        qbuf[lax.rem(pos[2] + 4 - d, 4)] = q[...]
    u = lax.broadcasted_iota(jnp.int32, (HEAD, 256), 0)
    t = lax.rem(lax.broadcasted_iota(jnp.int32, (HEAD, 256), 1), HEAD)
    for b in range(4):
        q = two_heads(qbuf[b, 0])
        qd = two_heads(qbuf[b, 1])
        q_all[b] = q
        keys = window_of(lines, b, slice(0, 256))
        values = window_of(lines, b, slice(256, 512))
        s = mm(keys[:, :HEAD], q, NT)
        split = (4 - b) * HEAD
        parts = [jnp.where(u > t, s[:HEAD] + far_bias, -1e30)]
        if b < 3:
            parts.append(s[HEAD:split] + far_bias)
        parts.append(s[split : split + 512] + near_bias)
        if b > 0:
            parts.append(s[split + 512 : 8 * HEAD])
        parts.append(jnp.where(u <= t, s[8 * HEAD :], -1e30))
        s = jnp.concatenate(parts, axis=0)
        e = jnp.exp2((s - jnp.max(s, axis=0, keepdims=True)) * SCALE2)
        inv = 1.0 / jnp.sum(e, axis=0, keepdims=True)
        sd = mm(keys, jnp.concatenate([qd, q], axis=1), NT)
        mean = jnp.sum(e * sd, axis=0, keepdims=True) * inv
        p_b = (e * inv).astype(BF)
        pd_b = (e * ((sd - mean) * (inv * SCALE))).astype(BF)
        p_all[b] = p_b
        mixed = mm(values[:, :HEAD], pd_b, TN) + mm(values[:, HEAD:], p_b, TN)
        obuf[b, :, :HEAD] = mixed[:, :HEAD].T.astype(BF)
        obuf[b, :, HEAD:] = mixed[:, HEAD:].T.astype(BF)
    for d, o in enumerate((o0, o1, o2, o3)):
        o[...] = obuf[lax.rem(pos[2] + d, 4)]


def place_heads(pos, chunks, buf, size):
    for d, c in enumerate(chunks):
        head = lax.rem(pos[2] + 4 - d, 4)
        buf[:, pl.ds(pl.multiple_of(head * size, size), size)] = c


def out_kernel(pos, o0, o1, o2, o3, w, total, sent, buf):
    place_heads(pos, (o0[...], o1[...], o2[...], o3[...]), buf, 256)
    full = mm(buf[...], w[...])
    total[...] = full
    sent[...] = full.astype(BF)


def gradient_kernel(pos, total, other, w, g0, g1, g2, g3, buf):
    ct = (total[...] + other[...].astype(F32)).astype(BF)
    buf[...] = mm(ct, w[...], NT).astype(BF)
    for d, ref in enumerate((g0, g1, g2, g3)):
        head = lax.rem(pos[2] + d, 4)
        ref[...] = buf[:, pl.ds(pl.multiple_of(head * 256, 256), 256)]


def backward_kernel(pos, g0, g1, g2, g3, low, high, near_kv, own_kv, q_all, p_all, *refs):
    q0, q1, q2, q3, own, near, far, dk, dv, gbuf, dqbuf = refs
    lines = (low, high, near_kv, own_kv)
    for d, g in enumerate((g0, g1, g2, g3)):
        gbuf[lax.rem(pos[2] + 4 - d, 4)] = g[...]
    for b in range(4):
        g = two_heads(gbuf[b])
        keys = window_of(lines, b, slice(0, HEAD))
        values = window_of(lines, b, slice(256, 384))
        p_b = p_all[b]
        dp = mm(values, g, NT)
        p = p_b.astype(F32)
        ds = (p * (dp - jnp.sum(p * dp, axis=0, keepdims=True))).astype(BF)
        dq = mm(keys, ds, TN) * SCALE
        dqbuf[b, :, :HEAD] = dq[:, :HEAD].T.astype(BF)
        dqbuf[b, :, HEAD:] = dq[:, HEAD:].T.astype(BF)
        dk_part = mm(ds, q_all[b])
        dv_part = mm(p_b, g)
        rows = slice(b * HEAD, b * HEAD + 9 * HEAD)
        if b == 0:
            dk[rows] = dk_part
            dv[rows] = dv_part
        else:
            fresh = slice(b * HEAD + 8 * HEAD, b * HEAD + 9 * HEAD)
            rows = slice(b * HEAD, b * HEAD + 8 * HEAD)
            dk[rows] += dk_part[: 8 * HEAD]
            dv[rows] += dv_part[: 8 * HEAD]
            dk[fresh] = dk_part[8 * HEAD :]
            dv[fresh] = dv_part[8 * HEAD :]
    far[:, :HEAD] = (dk[:512, :] * SCALE).astype(BF)
    far[:, HEAD:] = dv[:512, :].astype(BF)
    near[:, :HEAD] = (dk[512:1024, :] * SCALE).astype(BF)
    near[:, HEAD:] = dv[512:1024, :].astype(BF)
    own[:, :HEAD] = dk[1024:, :] * SCALE
    own[:, HEAD:] = dv[1024:, :]
    for d, q in enumerate((q0, q1, q2, q3)):
        q[...] = dqbuf[lax.rem(pos[2] + d, 4)]


def pair_kernel(pos, own, near, far, *outs):
    y = pos[2]
    for d in range(4):
        rows = pl.ds(pl.multiple_of(lax.rem(y + d, 4) * HEAD, HEAD), HEAD)
        outs[d][...] = (
            own[rows, :] + near[rows, :].astype(F32) + far[rows, :].astype(F32)
        ).astype(BF)


def query_input_kernel(pos, q0, q1, q2, q3, w, total, buf):
    place_heads(pos, (q0[...], q1[...], q2[...], q3[...]), buf, 256)
    total[...] = mm(w[...], buf[...], NT)


def pair_input_kernel(pos, c0, c1, c2, c3, base, wk, wv, kept, given, kbuf, vbuf, total):
    chunks = (c0, c1, c2, c3)
    place_heads(pos, [c[:, :HEAD] for c in chunks], kbuf, HEAD)
    place_heads(pos, [c[:, HEAD:] for c in chunks], vbuf, HEAD)
    total[...] = base[...] + (mm(wk[...], kbuf[...], NT) + mm(wv[...], vbuf[...], NT))
    half = kept.shape[0]
    kept[...] = total[pl.ds(pl.multiple_of(pos[3] * half, half), half), :]
    given[...] = total[pl.ds(pl.multiple_of((1 - pos[3]) * half, half), half), :].astype(BF)


def token_kernel(pos, mine, r1, r2, r3, p1, p2, p3, line, sems):
    half = r1.shape[0]
    copies = [pltpu.make_async_copy(mine, line.at[:, pl.ds(0, HEAD)], sems.at[0])]
    for d, (r, p) in enumerate(((r1, p1), (r2, p2), (r3, p3)), 1):
        for j, (src, where) in enumerate(((r, pos[3]), (p, 1 - pos[3]))):
            rows = pl.ds(pl.multiple_of(where * half, half), half)
            copies.append(
                pltpu.make_async_copy(
                    src, line.at[rows, pl.ds(d * HEAD, HEAD)], sems.at[2 * d - 1 + j]
                )
            )
    for c in copies:
        c.start()
    for c in copies:
        c.wait()


def weight_kernel(pos, line, c0, c1, c2, c3, *outs):
    pair = jnp.concatenate([c0[...], c3[...], c2[...], c1[...]], axis=0)
    size = 16 * PIECE
    for d in range(4):
        x = lax.rem(pos[0] + d, 4)
        block = line[pl.ds(pl.multiple_of(x * size, size), size), :]
        part = mm(block, pair).astype(BF)
        outs[d][...] = part


def add_up(ins, rows):
    total = ins[0][rows, :].astype(F32)
    for r in ins[1:]:
        total += r[rows, :].astype(F32)
    return total


def middle_kernel(pos, *refs):
    ins, outs, total = refs[:4], refs[4:8], refs[8]
    size = 4 * PIECE
    total[...] = add_up(ins, slice(None))
    for d in range(4):
        rows = pl.ds(pl.multiple_of(lax.rem(pos[1] + d, 4) * size, 8), size)
        outs[d][...] = total[rows, :].astype(BF)


def last_kernel(pos, *refs):
    ins, outs = refs[:4], refs[4:]
    total = add_up(ins, slice(None))
    parts = [total[i * PIECE : (i + 1) * PIECE] for i in range(4)]
    for d in range(4):
        at = lax.rem(pos[2] + d, 4)
        outs[d][...] = jnp.where(
            at < 2,
            jnp.where(at == 0, parts[0], parts[1]),
            jnp.where(at == 2, parts[2], parts[3]),
        )


def place_kernel(pos, c0, c1, c2, c3, res):
    for d, c in enumerate((c0, c1, c2, c3)):
        head = pl.multiple_of(lax.rem(pos[2] + 4 - d, 4) * HEAD, HEAD)
        for j in range(2):
            res[:, j, pl.ds(head, HEAD)] = c[: res.shape[0], j * HEAD : (j + 1) * HEAD]


def on_device(tokens, tangent, w_query, w_key, value_weight, w_out):
    rows, width = tokens.shape
    seq = lax.axis_index("seq")
    core = lax.axis_index("mp")
    pos = jnp.stack([seq // 16, seq // 4 % 4, seq % 4, core]).astype(jnp.int32)
    piece_out = [out((4, rows, HEAD), BF)] * 4
    tok_in = (far_memory(), tokens)
    tan_in = (far_memory(), tangent)
    kv = flat_call(
        key_value_kernel,
        [None, tok_in, tan_in, (far_memory(), w_key), (far_memory(), value_weight)],
        piece_out,
        [
            pltpu.VMEM((2 * rows, width), BF),
            pltpu.VMEM((width, 1024), BF),
            pltpu.VMEM((2 * rows, 1024), F32),
            pltpu.VMEM((2 * rows, 1024), BF),
            pltpu.SemaphoreType.DMA((10,)),
        ],
        flops=2 * 256 * width * 1024,
        moved=2 * width * 1024,
        limit=62,
    )
    line, low, high = flat_call(
        join_kernel,
        [pos] + [(vmem(), c) for c in exchange(ring_y, kv)],
        [out((512, 512), BF), out((256, 512), BF), out((256, 512), BF)],
        moved=1 << 20,
    )
    passed = far_one(high)
    near = lines_on(line, 1)
    far_low = lines_on(low, 2)
    far_high = far_two(passed)
    lines = [far_low, far_high, near, line]
    q = flat_call(
        query_kernel,
        [pos, (vmem(), tokens), (vmem(), tangent), (vmem(), w_query)],
        [out((2, rows, 256), BF)] * 4,
        [pltpu.VMEM((2 * rows, width), BF)],
        flops=2 * 256 * width * 1024,
        moved=2 * width * 1024,
    )
    late_tokens, _ = lax.optimization_barrier((tokens, q[0]))
    q = exchange(ring_y, q)
    columns = late_tokens.T
    half = lax.dynamic_slice_in_dim(columns, core * (width // 2), width // 2, 0)
    (w_out,) = flat_call(
        load_kernel,
        [pos, (far_memory(), w_out)],
        [out(w_out.shape, BF)],
        [pltpu.SemaphoreType.DMA],
        moved=2 * w_out.size,
    )
    halves = exchange(ring_y, [half] * 4)[1:]
    partner_halves = [other_core(h) for h in halves]

    attended = flat_call(
        forward_kernel,
        [pos] + [(vmem(), a) for a in lines + q],
        [out((rows, 256), BF)] * 4 + [out((4, 256, HEAD), BF), out((4, 1152, 256), BF)],
        [pltpu.VMEM((4, 2, rows, 256), BF), pltpu.VMEM((4, rows, 256), BF)],
        flops=2 * 4 * 1152 * 256 * 128 * 5,
        moved=8 << 20,
        limit=24,
    )
    o, (q_all, p_all) = attended[:4], attended[4:]
    o = exchange(ring_y, o)
    small = whole((rows, 256))
    wide = pltpu.VMEM((rows, 1024), BF)
    total, sent = flat_call(
        out_kernel,
        [pos] + [(vmem(), a) for a in o] + [(vmem(), w_out)],
        [out((rows, width), F32), out((rows, width), BF)],
        [wide],
        flops=2 * rows * width * 1024,
        moved=2 * width * 1024,
    )
    other = other_core(sent)
    g = flat_call(
        gradient_kernel,
        [pos, (vmem(), total), (vmem(), other), (vmem(), w_out)],
        [out((rows, 256), BF)] * 4,
        [wide],
        flops=2 * rows * width * 1024,
        moved=2 * width * 1024,
    )
    g = exchange(ring_y, g)
    back = flat_call(
        backward_kernel,
        [pos] + [(vmem(), a) for a in g + lines + [q_all, p_all]],
        [out((rows, 256), BF)] * 4 + [out((512, 256), F32), out((512, 256), BF), out((512, 256), BF)],
        [
            pltpu.VMEM((1536, HEAD), F32),
            pltpu.VMEM((1536, HEAD), F32),
            pltpu.VMEM((4, rows, 256), BF),
            pltpu.VMEM((4, rows, 256), BF),
        ],
        flops=2 * 4 * 1152 * 256 * 128 * 4,
        moved=6 << 20,
        limit=24,
    )
    dq, (own, to_near, to_far) = back[:4], back[4:]
    from_far = lines_on(to_far, -2)
    from_near = lines_on(to_near, -1)
    dq = exchange(ring_y, dq)
    pair = call(
        pair_kernel,
        (1,),
        [pos] + [(whole((512, 256)), a) for a in (own, from_near, from_far)],
        [out((rows, 256), BF)] * 4,
        moved=1 << 20,
    )
    mixed_pair = exchange(ring_y, pair)

    part = (16 * PIECE, 256)
    (token_line,) = flat_call(
        token_kernel,
        [pos] + [(hbm(), a) for a in [columns] + halves + partner_halves],
        [out((width, 512), BF)],
        [pltpu.SemaphoreType.DMA((7,))],
        moved=5 << 20,
    )
    stage = flat_call(
        weight_kernel,
        [pos, (vmem(), token_line)] + [(vmem(), a) for a in pair],
        [out(part, BF)] * 4,
        flops=2 * 2688 * 512 * 256,
        moved=5 << 20,
    )
    stage = exchange(ring_x, stage)
    stage = flat_call(
        middle_kernel,
        [pos] + [(vmem(), v) for v in stage],
        [out((4 * PIECE, 256), BF)] * 4,
        [pltpu.VMEM((16 * PIECE, 256), F32)],
        moved=2 << 20,
    )
    stage = exchange(ring_z, stage)
    stage = flat_call(
        last_kernel,
        [pos] + [(vmem(), v) for v in stage],
        [out((PIECE, 256), F32)] * 4,
        moved=1 << 19,
    )
    stage = exchange(ring_y, stage)
    (weight_grad,) = call(
        place_kernel,
        (1,),
        [pos] + [(whole((PIECE, 256)), v) for v in stage],
        [out((width // 64, 2, 512), F32)],
        moved=1 << 18,
    )

    (base,) = flat_call(
        query_input_kernel,
        [pos] + [(vmem(), a) for a in dq] + [(vmem(), w_query)],
        [out((width, rows), F32)],
        [wide],
        flops=2 * rows * width * 1024,
        moved=2 * width * 1024,
    )
    narrow = pltpu.VMEM((rows, 512), BF)
    kept, given = flat_call(
        pair_input_kernel,
        [pos]
        + [(vmem(), c) for c in mixed_pair]
        + [(vmem(), base), (vmem(), w_key), (vmem(), value_weight)],
        [out((width // 2, rows), F32), out((width // 2, rows), BF)],
        [narrow, narrow, pltpu.VMEM((width, rows), F32)],
        flops=2 * rows * width * 1024,
        moved=2 * width * 1024,
    )
    theirs = other_core(given)
    input_grad = (kept + theirs.astype(F32)).astype(BF).T
    return input_grad, weight_grad


def solution(mesh):
    placed = (
        P("seq", None),
        P("seq", None),
        P(None, "mp"),
        P(None, "mp"),
        P(None, "mp"),
        P("mp", None),
    )
    return jax.shard_map(
        on_device,
        mesh=mesh,
        in_specs=placed,
        out_specs=(P("seq", "mp"), P("seq", None, "mp")),
        check_vma=False,
    )
```

```python
import math

import jax
import jax.numpy as jnp
from jax import lax
from jax.experimental import pallas as pl
from jax.experimental.pallas import tpu as pltpu
from jax.sharding import PartitionSpec as P

BF = jnp.bfloat16
F32 = jnp.float32
HEAD = 128
SCALE = 168.0 ** (-0.5)
SCALE2 = SCALE * math.log2(math.e)
PIECE = 42


NT = (((1,), (1,)), ((), ()))
TN = (((0,), (0,)), ((), ()))
NN = (((1,), (0,)), ((), ()))


def mm(a, b, dims=NN):
    return lax.dot_general(a, b, dims, preferred_element_type=F32)


def ring_y(x, d):
    return lax.ppermute(x, "seq", [(i, i // 4 * 4 + (i + d) % 4) for i in range(64)])


def ring_z(x, d):
    return lax.ppermute(
        x, "seq", [(i, i // 16 * 16 + (i // 4 + d) % 4 * 4 + i % 4) for i in range(64)]
    )


def ring_x(x, d):
    return lax.ppermute(x, "seq", [(i, (i // 16 + d) % 4 * 16 + i % 16) for i in range(64)])


def lines_on(x, d):
    return lax.ppermute(x, "seq", [(i, (i + 4 * d) % 64) for i in range(64)])


def exchange(ring, chunks):
    got = {d: ring(chunks[d], d) for d in (1, 3, 2)}
    return [chunks[0], got[1], got[2], got[3]]


def far_one(x):
    return lax.ppermute(
        x, "seq", [(i, i // 16 * 16 + (i // 4 + 3) % 4 * 4 + i % 4) for i in range(64)]
    )


def far_two(x):
    route = []
    for i in range(64):
        source = i // 16 * 16 + (i // 4 + 1) % 4 * 4 + i % 4
        route.append((i, (source + 8) % 64))
    return lax.ppermute(x, "seq", route)


def other_core(x):
    return lax.ppermute(x, "mp", [(0, 1), (1, 0)])


def call(kernel, grid, ins, outs, scratch=(), flops=0, moved=0, limit=20):
    specs_in, values = zip(*ins[1:])
    specs_out, shapes = zip(*outs)
    return pl.pallas_call(
        kernel,
        grid_spec=pltpu.PrefetchScalarGridSpec(
            num_scalar_prefetch=1,
            grid=grid,
            in_specs=list(specs_in),
            out_specs=list(specs_out),
            scratch_shapes=list(scratch),
        ),
        out_shape=list(shapes),
        compiler_params=pltpu.CompilerParams(
            dimension_semantics=("arbitrary",) * len(grid), vmem_limit_bytes=limit << 20
        ),
        cost_estimate=pl.CostEstimate(flops=flops, bytes_accessed=moved, transcendentals=0),
    )(ins[0], *values)


def flat_call(kernel, ins, outs, scratch=(), flops=0, moved=0, limit=20):
    specs_in, values = zip(*ins[1:])
    if ins[0] is not None:
        specs_in = (pl.BlockSpec(memory_space=pltpu.SMEM),) + specs_in
        values = (ins[0],) + values
    _, shapes = zip(*outs)
    return pl.pallas_call(
        kernel,
        in_specs=list(specs_in),
        out_specs=[pl.BlockSpec(memory_space=pltpu.VMEM)] * len(shapes),
        scratch_shapes=list(scratch),
        out_shape=list(shapes),
        compiler_params=pltpu.CompilerParams(vmem_limit_bytes=limit << 20),
        cost_estimate=pl.CostEstimate(flops=flops, bytes_accessed=moved, transcendentals=0),
    )(*values)


def whole(shape):
    return pl.BlockSpec(shape, lambda *_: (0,) * len(shape))


def hbm():
    return pl.BlockSpec(memory_space=pl.ANY)


def far_memory():
    return pl.BlockSpec(memory_space=pltpu.HBM)


def vmem():
    return pl.BlockSpec(memory_space=pltpu.VMEM)


def out(shape, dtype):
    return whole(shape), jax.ShapeDtypeStruct(shape, dtype)


CUTS = (0, 512, 1152, 1920, 2688)


def key_value_kernel(tok, tan, wk, wv, *refs):
    y = lax.rem(lax.axis_index("seq"), 4)
    outs, (both, w, acc, flat, sem) = refs[:4], refs[4:]
    rows = tok.shape[0]
    half = wk.shape[1]
    copies = [
        pltpu.make_async_copy(tok, both.at[pl.ds(0, rows)], sem.at[0]),
        pltpu.make_async_copy(tan, both.at[pl.ds(rows, rows)], sem.at[1]),
    ]
    for j in range(4):
        part = pl.ds(CUTS[j], CUTS[j + 1] - CUTS[j])
        for i, src in enumerate((wk, wv)):
            copies.append(
                pltpu.make_async_copy(
                    src.at[part], w.at[part, pl.ds(i * half, half)], sem.at[2 + 2 * j + i]
                )
            )
    for c in copies[:6]:
        c.start()
    copies[0].wait()
    copies[1].wait()
    for j in range(4):
        copies[2 + 2 * j].wait()
        copies[3 + 2 * j].wait()
        for c in copies[6 + 2 * j : 8 + 2 * j]:
            c.start()
        part = slice(CUTS[j], CUTS[j + 1])
        res = mm(both[:, part], w[part, :])
        if j == 0:
            acc[...] = res
        elif j < 3:
            acc[...] += res
        else:
            flat[...] = (acc[...] + res).astype(BF)
    for d in range(4):
        head = lax.rem(y + d, 4) * HEAD
        k = flat[:, pl.ds(pl.multiple_of(head, HEAD), HEAD)]
        v = flat[:, pl.ds(pl.multiple_of(head + half, HEAD), HEAD)]
        outs[d][0] = k[:rows]
        outs[d][1] = k[rows:]
        outs[d][2] = v[:rows]
        outs[d][3] = v[rows:]


def query_kernel(pos, tok, tan, w, *refs):
    outs, both = refs[:4], refs[4]
    rows = tok.shape[0]
    both[:rows] = tok[...]
    both[rows:] = tan[...]
    for d in range(4):
        cols = pl.ds(pl.multiple_of(lax.rem(pos[2] + d, 4) * 256, 256), 256)
        res = mm(both[...], w[:, cols]).astype(BF)
        outs[d][0] = res[:rows]
        outs[d][1] = res[rows:]


def join_kernel(pos, a, b, c, e, line, low, high):
    for d, ref in enumerate((a, b, c, e)):
        block = lax.rem(pos[2] + 4 - d, 4)
        rows = pl.ds(pl.multiple_of(block * HEAD, HEAD), HEAD)
        for part in range(4):
            line[rows, part * HEAD : (part + 1) * HEAD] = ref[part]
    low[...] = line[: low.shape[0]]
    high[...] = line[low.shape[0] :]


def load_kernel(pos, src, dst, sem):
    copy = pltpu.make_async_copy(src, dst, sem)
    copy.start()
    copy.wait()


def two_heads(block):
    return jnp.concatenate([block[:, :HEAD], block[:, HEAD:]], axis=0)


def window_of(refs, b, cols):
    low, high, near, own = refs
    parts = []
    cut = low.shape[0] // HEAD
    if b < cut:
        parts.append(low[b * HEAD :, cols])
        parts.append(high[:, cols])
    else:
        parts.append(high[(b - cut) * HEAD :, cols])
    parts += [near[:, cols], own[: (b + 1) * HEAD, cols]]
    return jnp.concatenate(parts, axis=0)


def forward_kernel(pos, low, high, near, own, q0, q1, q2, q3, *refs):
    o0, o1, o2, o3, q_all, p_all, qbuf, obuf = refs
    lines = (low, high, near, own)
    line = 4 * pos[0] + pos[1]
    far_bias = jnp.where(line < 2, -1e30, 0.0).astype(F32)
    near_bias = jnp.where(line < 1, -1e30, 0.0).astype(F32)
    for d, q in enumerate((q0, q1, q2, q3)):
        qbuf[lax.rem(pos[2] + 4 - d, 4)] = q[...]
    u = lax.broadcasted_iota(jnp.int32, (HEAD, 256), 0)
    t = lax.rem(lax.broadcasted_iota(jnp.int32, (HEAD, 256), 1), HEAD)
    for b in range(4):
        q = two_heads(qbuf[b, 0])
        qd = two_heads(qbuf[b, 1])
        q_all[b] = q
        keys = window_of(lines, b, slice(0, 256))
        values = window_of(lines, b, slice(256, 512))
        s = mm(keys[:, :HEAD], q, NT)
        split = (4 - b) * HEAD
        parts = [jnp.where(u > t, s[:HEAD] + far_bias, -1e30)]
        if b < 3:
            parts.append(s[HEAD:split] + far_bias)
        parts.append(s[split : split + 512] + near_bias)
        if b > 0:
            parts.append(s[split + 512 : 8 * HEAD])
        parts.append(jnp.where(u <= t, s[8 * HEAD :], -1e30))
        s = jnp.concatenate(parts, axis=0)
        e = jnp.exp2((s - jnp.max(s, axis=0, keepdims=True)) * SCALE2)
        inv = 1.0 / jnp.sum(e, axis=0, keepdims=True)
        sd = mm(keys, jnp.concatenate([qd, q], axis=1), NT)
        mean = jnp.sum(e * sd, axis=0, keepdims=True) * inv
        p_b = (e * inv).astype(BF)
        pd_b = (e * ((sd - mean) * (inv * SCALE))).astype(BF)
        p_all[b] = p_b
        mixed = mm(values[:, :HEAD], pd_b, TN) + mm(values[:, HEAD:], p_b, TN)
        obuf[b, :, :HEAD] = mixed[:, :HEAD].T.astype(BF)
        obuf[b, :, HEAD:] = mixed[:, HEAD:].T.astype(BF)
    for d, o in enumerate((o0, o1, o2, o3)):
        o[...] = obuf[lax.rem(pos[2] + d, 4)]


def place_heads(pos, chunks, buf, size):
    for d, c in enumerate(chunks):
        head = lax.rem(pos[2] + 4 - d, 4)
        buf[:, pl.ds(pl.multiple_of(head * size, size), size)] = c


def out_kernel(pos, o0, o1, o2, o3, w, total, sent, buf):
    place_heads(pos, (o0[...], o1[...], o2[...], o3[...]), buf, 256)
    full = mm(buf[...], w[...])
    total[...] = full
    sent[...] = full.astype(BF)


def gradient_kernel(pos, total, other, w, g0, g1, g2, g3, buf):
    ct = (total[...] + other[...].astype(F32)).astype(BF)
    buf[...] = mm(ct, w[...], NT).astype(BF)
    for d, ref in enumerate((g0, g1, g2, g3)):
        head = lax.rem(pos[2] + d, 4)
        ref[...] = buf[:, pl.ds(pl.multiple_of(head * 256, 256), 256)]


def backward_kernel(pos, g0, g1, g2, g3, low, high, near_kv, own_kv, q_all, p_all, *refs):
    q0, q1, q2, q3, own, near, far, dk, dv, gbuf, dqbuf = refs
    lines = (low, high, near_kv, own_kv)
    for d, g in enumerate((g0, g1, g2, g3)):
        gbuf[lax.rem(pos[2] + 4 - d, 4)] = g[...]
    for b in range(4):
        g = two_heads(gbuf[b])
        keys = window_of(lines, b, slice(0, HEAD))
        values = window_of(lines, b, slice(256, 384))
        p_b = p_all[b]
        dp = mm(values, g, NT)
        p = p_b.astype(F32)
        ds = (p * (dp - jnp.sum(p * dp, axis=0, keepdims=True))).astype(BF)
        dq = mm(keys, ds, TN) * SCALE
        dqbuf[b, :, :HEAD] = dq[:, :HEAD].T.astype(BF)
        dqbuf[b, :, HEAD:] = dq[:, HEAD:].T.astype(BF)
        dk_part = mm(ds, q_all[b])
        dv_part = mm(p_b, g)
        rows = slice(b * HEAD, b * HEAD + 9 * HEAD)
        if b == 0:
            dk[rows] = dk_part
            dv[rows] = dv_part
        else:
            fresh = slice(b * HEAD + 8 * HEAD, b * HEAD + 9 * HEAD)
            rows = slice(b * HEAD, b * HEAD + 8 * HEAD)
            dk[rows] += dk_part[: 8 * HEAD]
            dv[rows] += dv_part[: 8 * HEAD]
            dk[fresh] = dk_part[8 * HEAD :]
            dv[fresh] = dv_part[8 * HEAD :]
    far[:, :HEAD] = (dk[:512, :] * SCALE).astype(BF)
    far[:, HEAD:] = dv[:512, :].astype(BF)
    near[:, :HEAD] = (dk[512:1024, :] * SCALE).astype(BF)
    near[:, HEAD:] = dv[512:1024, :].astype(BF)
    own[:, :HEAD] = dk[1024:, :] * SCALE
    own[:, HEAD:] = dv[1024:, :]
    for d, q in enumerate((q0, q1, q2, q3)):
        q[...] = dqbuf[lax.rem(pos[2] + d, 4)]


def pair_kernel(pos, own, near, far, *outs):
    y = pos[2]
    for d in range(4):
        rows = pl.ds(pl.multiple_of(lax.rem(y + d, 4) * HEAD, HEAD), HEAD)
        outs[d][...] = (
            own[rows, :] + near[rows, :].astype(F32) + far[rows, :].astype(F32)
        ).astype(BF)


def query_input_kernel(pos, q0, q1, q2, q3, w, total, buf):
    place_heads(pos, (q0[...], q1[...], q2[...], q3[...]), buf, 256)
    total[...] = mm(w[...], buf[...], NT)


def pair_input_kernel(pos, c0, c1, c2, c3, base, wk, wv, kept, given, kbuf, vbuf, total):
    chunks = (c0, c1, c2, c3)
    place_heads(pos, [c[:, :HEAD] for c in chunks], kbuf, HEAD)
    place_heads(pos, [c[:, HEAD:] for c in chunks], vbuf, HEAD)
    total[...] = base[...] + (mm(wk[...], kbuf[...], NT) + mm(wv[...], vbuf[...], NT))
    half = kept.shape[0]
    kept[...] = total[pl.ds(pl.multiple_of(pos[3] * half, half), half), :]
    given[...] = total[pl.ds(pl.multiple_of((1 - pos[3]) * half, half), half), :].astype(BF)


def token_kernel(pos, mine, r1, r2, r3, p1, p2, p3, line, sems):
    half = r1.shape[0]
    copies = [pltpu.make_async_copy(mine, line.at[:, pl.ds(0, HEAD)], sems.at[0])]
    for d, (r, p) in enumerate(((r1, p1), (r2, p2), (r3, p3)), 1):
        for j, (src, where) in enumerate(((r, pos[3]), (p, 1 - pos[3]))):
            rows = pl.ds(pl.multiple_of(where * half, half), half)
            copies.append(
                pltpu.make_async_copy(
                    src, line.at[rows, pl.ds(d * HEAD, HEAD)], sems.at[2 * d - 1 + j]
                )
            )
    for c in copies:
        c.start()
    for c in copies:
        c.wait()


def weight_kernel(pos, line, c0, c1, c2, c3, *outs):
    pair = jnp.concatenate([c0[...], c3[...], c2[...], c1[...]], axis=0)
    size = 16 * PIECE
    for d in range(4):
        x = lax.rem(pos[0] + d, 4)
        block = line[pl.ds(pl.multiple_of(x * size, size), size), :]
        part = mm(block, pair).astype(BF)
        outs[d][...] = part


def add_up(ins, rows):
    total = ins[0][rows, :].astype(F32)
    for r in ins[1:]:
        total += r[rows, :].astype(F32)
    return total


def middle_kernel(pos, *refs):
    ins, outs, total = refs[:4], refs[4:8], refs[8]
    size = 4 * PIECE
    total[...] = add_up(ins, slice(None))
    for d in range(4):
        rows = pl.ds(pl.multiple_of(lax.rem(pos[1] + d, 4) * size, 8), size)
        outs[d][...] = total[rows, :].astype(BF)


def last_kernel(pos, *refs):
    ins, outs = refs[:4], refs[4:]
    total = add_up(ins, slice(None))
    parts = [total[i * PIECE : (i + 1) * PIECE] for i in range(4)]
    for d in range(4):
        at = lax.rem(pos[2] + d, 4)
        outs[d][...] = jnp.where(
            at < 2,
            jnp.where(at == 0, parts[0], parts[1]),
            jnp.where(at == 2, parts[2], parts[3]),
        )


def place_kernel(pos, c0, c1, c2, c3, res):
    for d, c in enumerate((c0, c1, c2, c3)):
        head = pl.multiple_of(lax.rem(pos[2] + 4 - d, 4) * HEAD, HEAD)
        for j in range(2):
            res[:, j, pl.ds(head, HEAD)] = c[: res.shape[0], j * HEAD : (j + 1) * HEAD]


def on_device(tokens, tangent, w_query, w_key, value_weight, w_out):
    rows, width = tokens.shape
    seq = lax.axis_index("seq")
    core = lax.axis_index("mp")
    pos = jnp.stack([seq // 16, seq // 4 % 4, seq % 4, core]).astype(jnp.int32)
    piece_out = [out((4, rows, HEAD), BF)] * 4
    tok_in = (far_memory(), tokens)
    tan_in = (far_memory(), tangent)
    kv = flat_call(
        key_value_kernel,
        [None, tok_in, tan_in, (far_memory(), w_key), (far_memory(), value_weight)],
        piece_out,
        [
            pltpu.VMEM((2 * rows, width), BF),
            pltpu.VMEM((width, 1024), BF),
            pltpu.VMEM((2 * rows, 1024), F32),
            pltpu.VMEM((2 * rows, 1024), BF),
            pltpu.SemaphoreType.DMA((10,)),
        ],
        flops=2 * 256 * width * 1024,
        moved=2 * width * 1024,
        limit=62,
    )
    line, low, high = flat_call(
        join_kernel,
        [pos] + [(vmem(), c) for c in exchange(ring_y, kv)],
        [out((512, 512), BF), out((128, 512), BF), out((384, 512), BF)],
        moved=1 << 20,
    )
    passed = far_one(high)
    near = lines_on(line, 1)
    far_low = lines_on(low, 2)
    far_high = far_two(passed)
    lines = [far_low, far_high, near, line]
    q = flat_call(
        query_kernel,
        [pos, (vmem(), tokens), (vmem(), tangent), (vmem(), w_query)],
        [out((2, rows, 256), BF)] * 4,
        [pltpu.VMEM((2 * rows, width), BF)],
        flops=2 * 256 * width * 1024,
        moved=2 * width * 1024,
    )
    late_tokens, _ = lax.optimization_barrier((tokens, q[0]))
    q = exchange(ring_y, q)
    columns = late_tokens.T
    half = lax.dynamic_slice_in_dim(columns, core * (width // 2), width // 2, 0)
    (w_out,) = flat_call(
        load_kernel,
        [pos, (far_memory(), w_out)],
        [out(w_out.shape, BF)],
        [pltpu.SemaphoreType.DMA],
        moved=2 * w_out.size,
    )
    halves = exchange(ring_y, [half] * 4)[1:]
    partner_halves = [other_core(h) for h in halves]

    attended = flat_call(
        forward_kernel,
        [pos] + [(vmem(), a) for a in lines + q],
        [out((rows, 256), BF)] * 4 + [out((4, 256, HEAD), BF), out((4, 1152, 256), BF)],
        [pltpu.VMEM((4, 2, rows, 256), BF), pltpu.VMEM((4, rows, 256), BF)],
        flops=2 * 4 * 1152 * 256 * 128 * 5,
        moved=8 << 20,
        limit=24,
    )
    o, (q_all, p_all) = attended[:4], attended[4:]
    o = exchange(ring_y, o)
    small = whole((rows, 256))
    wide = pltpu.VMEM((rows, 1024), BF)
    total, sent = flat_call(
        out_kernel,
        [pos] + [(vmem(), a) for a in o] + [(vmem(), w_out)],
        [out((rows, width), F32), out((rows, width), BF)],
        [wide],
        flops=2 * rows * width * 1024,
        moved=2 * width * 1024,
    )
    other = other_core(sent)
    g = flat_call(
        gradient_kernel,
        [pos, (vmem(), total), (vmem(), other), (vmem(), w_out)],
        [out((rows, 256), BF)] * 4,
        [wide],
        flops=2 * rows * width * 1024,
        moved=2 * width * 1024,
    )
    g = exchange(ring_y, g)
    back = flat_call(
        backward_kernel,
        [pos] + [(vmem(), a) for a in g + lines + [q_all, p_all]],
        [out((rows, 256), BF)] * 4 + [out((512, 256), F32), out((512, 256), BF), out((512, 256), BF)],
        [
            pltpu.VMEM((1536, HEAD), F32),
            pltpu.VMEM((1536, HEAD), F32),
            pltpu.VMEM((4, rows, 256), BF),
            pltpu.VMEM((4, rows, 256), BF),
        ],
        flops=2 * 4 * 1152 * 256 * 128 * 4,
        moved=6 << 20,
        limit=24,
    )
    dq, (own, to_near, to_far) = back[:4], back[4:]
    from_far = lines_on(to_far, -2)
    from_near = lines_on(to_near, -1)
    dq = exchange(ring_y, dq)
    pair = call(
        pair_kernel,
        (1,),
        [pos] + [(whole((512, 256)), a) for a in (own, from_near, from_far)],
        [out((rows, 256), BF)] * 4,
        moved=1 << 20,
    )
    mixed_pair = exchange(ring_y, pair)

    part = (16 * PIECE, 256)
    (token_line,) = flat_call(
        token_kernel,
        [pos] + [(hbm(), a) for a in [columns] + halves + partner_halves],
        [out((width, 512), BF)],
        [pltpu.SemaphoreType.DMA((7,))],
        moved=5 << 20,
    )
    stage = flat_call(
        weight_kernel,
        [pos, (vmem(), token_line)] + [(vmem(), a) for a in pair],
        [out(part, BF)] * 4,
        flops=2 * 2688 * 512 * 256,
        moved=5 << 20,
    )
    stage = exchange(ring_x, stage)
    stage = flat_call(
        middle_kernel,
        [pos] + [(vmem(), v) for v in stage],
        [out((4 * PIECE, 256), BF)] * 4,
        [pltpu.VMEM((16 * PIECE, 256), F32)],
        moved=2 << 20,
    )
    stage = exchange(ring_z, stage)
    stage = flat_call(
        last_kernel,
        [pos] + [(vmem(), v) for v in stage],
        [out((PIECE, 256), F32)] * 4,
        moved=1 << 19,
    )
    stage = exchange(ring_y, stage)
    (weight_grad,) = call(
        place_kernel,
        (1,),
        [pos] + [(whole((PIECE, 256)), v) for v in stage],
        [out((width // 64, 2, 512), F32)],
        moved=1 << 18,
    )

    (base,) = flat_call(
        query_input_kernel,
        [pos] + [(vmem(), a) for a in dq] + [(vmem(), w_query)],
        [out((width, rows), F32)],
        [wide],
        flops=2 * rows * width * 1024,
        moved=2 * width * 1024,
    )
    narrow = pltpu.VMEM((rows, 512), BF)
    kept, given = flat_call(
        pair_input_kernel,
        [pos]
        + [(vmem(), c) for c in mixed_pair]
        + [(vmem(), base), (vmem(), w_key), (vmem(), value_weight)],
        [out((width // 2, rows), F32), out((width // 2, rows), BF)],
        [narrow, narrow, pltpu.VMEM((width, rows), F32)],
        flops=2 * rows * width * 1024,
        moved=2 * width * 1024,
    )
    theirs = other_core(given)
    input_grad = (kept + theirs.astype(F32)).astype(BF).T
    return input_grad, weight_grad


def solution(mesh):
    placed = (
        P("seq", None),
        P("seq", None),
        P(None, "mp"),
        P(None, "mp"),
        P(None, "mp"),
        P("mp", None),
    )
    return jax.shard_map(
        on_device,
        mesh=mesh,
        in_specs=placed,
        out_specs=(P("seq", "mp"), P("seq", None, "mp")),
        check_vma=False,
    )
```

```python
import math

import jax
import jax.numpy as jnp
from jax import lax
from jax.experimental import pallas as pl
from jax.experimental.pallas import tpu as pltpu
from jax.sharding import PartitionSpec as P

BF = jnp.bfloat16
F32 = jnp.float32
HEAD = 128
SCALE = 168.0 ** (-0.5)
SCALE2 = SCALE * math.log2(math.e)
PIECE = 42


NT = (((1,), (1,)), ((), ()))
TN = (((0,), (0,)), ((), ()))
NN = (((1,), (0,)), ((), ()))


def mm(a, b, dims=NN):
    return lax.dot_general(a, b, dims, preferred_element_type=F32)


def ring_y(x, d):
    return lax.ppermute(x, "seq", [(i, i // 4 * 4 + (i + d) % 4) for i in range(64)])


def ring_z(x, d):
    return lax.ppermute(
        x, "seq", [(i, i // 16 * 16 + (i // 4 + d) % 4 * 4 + i % 4) for i in range(64)]
    )


def ring_x(x, d):
    return lax.ppermute(x, "seq", [(i, (i // 16 + d) % 4 * 16 + i % 16) for i in range(64)])


def lines_on(x, d):
    return lax.ppermute(x, "seq", [(i, (i + 4 * d) % 64) for i in range(64)])


def exchange(ring, chunks):
    got = {d: ring(chunks[d], d) for d in (1, 3, 2)}
    return [chunks[0], got[1], got[2], got[3]]


def far_one(x):
    return lax.ppermute(
        x, "seq", [(i, i // 16 * 16 + (i // 4 + 3) % 4 * 4 + i % 4) for i in range(64)]
    )


def far_two(x):
    route = []
    for i in range(64):
        source = i // 16 * 16 + (i // 4 + 1) % 4 * 4 + i % 4
        route.append((i, (source + 8) % 64))
    return lax.ppermute(x, "seq", route)


def back_one(x):
    return lax.ppermute(
        x, "seq", [(i, i // 16 * 16 + (i // 4 + 1) % 4 * 4 + i % 4) for i in range(64)]
    )


def back_two(x):
    route = []
    for i in range(64):
        source = i // 16 * 16 + (i // 4 + 3) % 4 * 4 + i % 4
        route.append((i, (source - 8) % 64))
    return lax.ppermute(x, "seq", route)


def other_core(x):
    return lax.ppermute(x, "mp", [(0, 1), (1, 0)])


def call(kernel, grid, ins, outs, scratch=(), flops=0, moved=0, limit=20):
    specs_in, values = zip(*ins[1:])
    specs_out, shapes = zip(*outs)
    return pl.pallas_call(
        kernel,
        grid_spec=pltpu.PrefetchScalarGridSpec(
            num_scalar_prefetch=1,
            grid=grid,
            in_specs=list(specs_in),
            out_specs=list(specs_out),
            scratch_shapes=list(scratch),
        ),
        out_shape=list(shapes),
        compiler_params=pltpu.CompilerParams(
            dimension_semantics=("arbitrary",) * len(grid), vmem_limit_bytes=limit << 20
        ),
        cost_estimate=pl.CostEstimate(flops=flops, bytes_accessed=moved, transcendentals=0),
    )(ins[0], *values)


def flat_call(kernel, ins, outs, scratch=(), flops=0, moved=0, limit=20):
    specs_in, values = zip(*ins[1:])
    if ins[0] is not None:
        specs_in = (pl.BlockSpec(memory_space=pltpu.SMEM),) + specs_in
        values = (ins[0],) + values
    _, shapes = zip(*outs)
    return pl.pallas_call(
        kernel,
        in_specs=list(specs_in),
        out_specs=[pl.BlockSpec(memory_space=pltpu.VMEM)] * len(shapes),
        scratch_shapes=list(scratch),
        out_shape=list(shapes),
        compiler_params=pltpu.CompilerParams(vmem_limit_bytes=limit << 20),
        cost_estimate=pl.CostEstimate(flops=flops, bytes_accessed=moved, transcendentals=0),
    )(*values)


def whole(shape):
    return pl.BlockSpec(shape, lambda *_: (0,) * len(shape))


def hbm():
    return pl.BlockSpec(memory_space=pl.ANY)


def far_memory():
    return pl.BlockSpec(memory_space=pltpu.HBM)


def vmem():
    return pl.BlockSpec(memory_space=pltpu.VMEM)


def out(shape, dtype):
    return whole(shape), jax.ShapeDtypeStruct(shape, dtype)


CUTS = (0, 512, 1152, 1920, 2688)


def key_value_kernel(tok, tan, wk, wv, *refs):
    y = lax.rem(lax.axis_index("seq"), 4)
    outs, (both, w, acc, flat, sem) = refs[:4], refs[4:]
    rows = tok.shape[0]
    half = wk.shape[1]
    copies = [
        pltpu.make_async_copy(tok, both.at[pl.ds(0, rows)], sem.at[0]),
        pltpu.make_async_copy(tan, both.at[pl.ds(rows, rows)], sem.at[1]),
    ]
    for j in range(4):
        part = pl.ds(CUTS[j], CUTS[j + 1] - CUTS[j])
        for i, src in enumerate((wk, wv)):
            copies.append(
                pltpu.make_async_copy(
                    src.at[part], w.at[part, pl.ds(i * half, half)], sem.at[2 + 2 * j + i]
                )
            )
    for c in copies[:6]:
        c.start()
    copies[0].wait()
    copies[1].wait()
    for j in range(4):
        copies[2 + 2 * j].wait()
        copies[3 + 2 * j].wait()
        for c in copies[6 + 2 * j : 8 + 2 * j]:
            c.start()
        part = slice(CUTS[j], CUTS[j + 1])
        res = mm(both[:, part], w[part, :])
        if j == 0:
            acc[...] = res
        elif j < 3:
            acc[...] += res
        else:
            flat[...] = (acc[...] + res).astype(BF)
    for d in range(4):
        head = lax.rem(y + d, 4) * HEAD
        k = flat[:, pl.ds(pl.multiple_of(head, HEAD), HEAD)]
        v = flat[:, pl.ds(pl.multiple_of(head + half, HEAD), HEAD)]
        outs[d][0] = k[:rows]
        outs[d][1] = k[rows:]
        outs[d][2] = v[:rows]
        outs[d][3] = v[rows:]


def query_kernel(pos, tok, tan, w, *refs):
    outs, both = refs[:4], refs[4]
    rows = tok.shape[0]
    both[:rows] = tok[...]
    both[rows:] = tan[...]
    for d in range(4):
        cols = pl.ds(pl.multiple_of(lax.rem(pos[2] + d, 4) * 256, 256), 256)
        res = mm(both[...], w[:, cols]).astype(BF)
        outs[d][0] = res[:rows]
        outs[d][1] = res[rows:]


def join_kernel(pos, a, b, c, e, line, low, high):
    for d, ref in enumerate((a, b, c, e)):
        block = lax.rem(pos[2] + 4 - d, 4)
        rows = pl.ds(pl.multiple_of(block * HEAD, HEAD), HEAD)
        for part in range(4):
            line[rows, part * HEAD : (part + 1) * HEAD] = ref[part]
    low[...] = line[: low.shape[0]]
    high[...] = line[low.shape[0] :]


def load_kernel(pos, src, dst, sem):
    copy = pltpu.make_async_copy(src, dst, sem)
    copy.start()
    copy.wait()


def two_heads(block):
    return jnp.concatenate([block[:, :HEAD], block[:, HEAD:]], axis=0)


def window_of(refs, b, cols):
    low, high, near, own = refs
    parts = []
    cut = low.shape[0] // HEAD
    if b < cut:
        parts.append(low[b * HEAD :, cols])
        parts.append(high[:, cols])
    else:
        parts.append(high[(b - cut) * HEAD :, cols])
    parts += [near[:, cols], own[: (b + 1) * HEAD, cols]]
    return jnp.concatenate(parts, axis=0)


def forward_kernel(pos, low, high, near, own, q0, q1, q2, q3, *refs):
    o0, o1, o2, o3, q_all, p_all, qbuf, obuf = refs
    lines = (low, high, near, own)
    line = 4 * pos[0] + pos[1]
    far_bias = jnp.where(line < 2, -1e30, 0.0).astype(F32)
    near_bias = jnp.where(line < 1, -1e30, 0.0).astype(F32)
    for d, q in enumerate((q0, q1, q2, q3)):
        qbuf[lax.rem(pos[2] + 4 - d, 4)] = q[...]
    u = lax.broadcasted_iota(jnp.int32, (HEAD, 256), 0)
    t = lax.rem(lax.broadcasted_iota(jnp.int32, (HEAD, 256), 1), HEAD)
    for b in range(4):
        q = two_heads(qbuf[b, 0])
        qd = two_heads(qbuf[b, 1])
        q_all[b] = q
        keys = window_of(lines, b, slice(0, 256))
        values = window_of(lines, b, slice(256, 512))
        s = mm(keys[:, :HEAD], q, NT)
        split = (4 - b) * HEAD
        parts = [jnp.where(u > t, s[:HEAD] + far_bias, -1e30)]
        if b < 3:
            parts.append(s[HEAD:split] + far_bias)
        parts.append(s[split : split + 512] + near_bias)
        if b > 0:
            parts.append(s[split + 512 : 8 * HEAD])
        parts.append(jnp.where(u <= t, s[8 * HEAD :], -1e30))
        s = jnp.concatenate(parts, axis=0)
        e = jnp.exp2((s - jnp.max(s, axis=0, keepdims=True)) * SCALE2)
        inv = 1.0 / jnp.sum(e, axis=0, keepdims=True)
        sd = mm(keys, jnp.concatenate([qd, q], axis=1), NT)
        mean = jnp.sum(e * sd, axis=0, keepdims=True) * inv
        p_b = (e * inv).astype(BF)
        pd_b = (e * ((sd - mean) * (inv * SCALE))).astype(BF)
        p_all[b] = p_b
        mixed = mm(values[:, :HEAD], pd_b, TN) + mm(values[:, HEAD:], p_b, TN)
        obuf[b, :, :HEAD] = mixed[:, :HEAD].T.astype(BF)
        obuf[b, :, HEAD:] = mixed[:, HEAD:].T.astype(BF)
    for d, o in enumerate((o0, o1, o2, o3)):
        o[...] = obuf[lax.rem(pos[2] + d, 4)]


def place_heads(pos, chunks, buf, size):
    for d, c in enumerate(chunks):
        head = lax.rem(pos[2] + 4 - d, 4)
        buf[:, pl.ds(pl.multiple_of(head * size, size), size)] = c


def out_kernel(pos, o0, o1, o2, o3, w, total, sent, buf):
    place_heads(pos, (o0[...], o1[...], o2[...], o3[...]), buf, 256)
    full = mm(buf[...], w[...])
    total[...] = full
    sent[...] = full.astype(BF)


def gradient_kernel(pos, total, other, w, g0, g1, g2, g3, buf):
    ct = (total[...] + other[...].astype(F32)).astype(BF)
    buf[...] = mm(ct, w[...], NT).astype(BF)
    for d, ref in enumerate((g0, g1, g2, g3)):
        head = lax.rem(pos[2] + d, 4)
        ref[...] = buf[:, pl.ds(pl.multiple_of(head * 256, 256), 256)]


def backward_kernel(pos, g0, g1, g2, g3, low, high, near_kv, own_kv, q_all, p_all, *refs):
    q0, q1, q2, q3, own, near, far_low, far_high, dk, dv, gbuf, dqbuf = refs
    lines = (low, high, near_kv, own_kv)
    for d, g in enumerate((g0, g1, g2, g3)):
        gbuf[lax.rem(pos[2] + 4 - d, 4)] = g[...]
    for b in range(4):
        g = two_heads(gbuf[b])
        keys = window_of(lines, b, slice(0, HEAD))
        values = window_of(lines, b, slice(256, 384))
        p_b = p_all[b]
        dp = mm(values, g, NT)
        p = p_b.astype(F32)
        ds = (p * (dp - jnp.sum(p * dp, axis=0, keepdims=True))).astype(BF)
        dq = mm(keys, ds, TN) * SCALE
        dqbuf[b, :, :HEAD] = dq[:, :HEAD].T.astype(BF)
        dqbuf[b, :, HEAD:] = dq[:, HEAD:].T.astype(BF)
        dk_part = mm(ds, q_all[b])
        dv_part = mm(p_b, g)
        rows = slice(b * HEAD, b * HEAD + 9 * HEAD)
        if b == 0:
            dk[rows] = dk_part
            dv[rows] = dv_part
        else:
            fresh = slice(b * HEAD + 8 * HEAD, b * HEAD + 9 * HEAD)
            rows = slice(b * HEAD, b * HEAD + 8 * HEAD)
            dk[rows] += dk_part[: 8 * HEAD]
            dv[rows] += dv_part[: 8 * HEAD]
            dk[fresh] = dk_part[8 * HEAD :]
            dv[fresh] = dv_part[8 * HEAD :]
    for i, far in enumerate((far_low, far_high)):
        rows = slice(i * 256, i * 256 + 256)
        far[:, :HEAD] = (dk[rows, :] * SCALE).astype(BF)
        far[:, HEAD:] = dv[rows, :].astype(BF)
    near[:, :HEAD] = (dk[512:1024, :] * SCALE).astype(BF)
    near[:, HEAD:] = dv[512:1024, :].astype(BF)
    own[:, :HEAD] = dk[1024:, :] * SCALE
    own[:, HEAD:] = dv[1024:, :]
    for d, q in enumerate((q0, q1, q2, q3)):
        q[...] = dqbuf[lax.rem(pos[2] + d, 4)]


def pair_kernel(pos, own, near, low, high, *outs):
    y = pos[2]
    for d in range(4):
        rows = pl.ds(pl.multiple_of(lax.rem(y + d, 4) * HEAD, HEAD), HEAD)
        block = lax.rem(y + d, 4)
        half = pl.ds(pl.multiple_of(lax.rem(block, 2) * HEAD, HEAD), HEAD)
        far = jnp.where(block < 2, low[half, :].astype(F32), high[half, :].astype(F32))
        outs[d][...] = (own[rows, :] + near[rows, :].astype(F32) + far).astype(BF)


def query_input_kernel(pos, q0, q1, q2, q3, w, total, buf):
    place_heads(pos, (q0[...], q1[...], q2[...], q3[...]), buf, 256)
    total[...] = mm(w[...], buf[...], NT)


def pair_input_kernel(pos, c0, c1, c2, c3, base, wk, wv, kept, given, kbuf, vbuf, total):
    chunks = (c0, c1, c2, c3)
    place_heads(pos, [c[:, :HEAD] for c in chunks], kbuf, HEAD)
    place_heads(pos, [c[:, HEAD:] for c in chunks], vbuf, HEAD)
    total[...] = base[...] + (mm(wk[...], kbuf[...], NT) + mm(wv[...], vbuf[...], NT))
    half = kept.shape[0]
    kept[...] = total[pl.ds(pl.multiple_of(pos[3] * half, half), half), :]
    given[...] = total[pl.ds(pl.multiple_of((1 - pos[3]) * half, half), half), :].astype(BF)


def token_kernel(pos, mine, r1, r2, r3, p1, p2, p3, line, sems):
    half = r1.shape[0]
    copies = [pltpu.make_async_copy(mine, line.at[:, pl.ds(0, HEAD)], sems.at[0])]
    for d, (r, p) in enumerate(((r1, p1), (r2, p2), (r3, p3)), 1):
        for j, (src, where) in enumerate(((r, pos[3]), (p, 1 - pos[3]))):
            rows = pl.ds(pl.multiple_of(where * half, half), half)
            copies.append(
                pltpu.make_async_copy(
                    src, line.at[rows, pl.ds(d * HEAD, HEAD)], sems.at[2 * d - 1 + j]
                )
            )
    for c in copies:
        c.start()
    for c in copies:
        c.wait()


def weight_kernel(pos, line, c0, c1, c2, c3, *outs):
    pair = jnp.concatenate([c0[...], c3[...], c2[...], c1[...]], axis=0)
    size = 16 * PIECE
    for d in range(4):
        x = lax.rem(pos[0] + d, 4)
        block = line[pl.ds(pl.multiple_of(x * size, size), size), :]
        part = mm(block, pair).astype(BF)
        outs[d][...] = part


def add_up(ins, rows):
    total = ins[0][rows, :].astype(F32)
    for r in ins[1:]:
        total += r[rows, :].astype(F32)
    return total


def middle_kernel(pos, *refs):
    ins, outs, total = refs[:4], refs[4:8], refs[8]
    size = 4 * PIECE
    total[...] = add_up(ins, slice(None))
    for d in range(4):
        rows = pl.ds(pl.multiple_of(lax.rem(pos[1] + d, 4) * size, 8), size)
        outs[d][...] = total[rows, :].astype(BF)


def last_kernel(pos, *refs):
    ins, outs = refs[:4], refs[4:]
    total = add_up(ins, slice(None))
    parts = [total[i * PIECE : (i + 1) * PIECE] for i in range(4)]
    for d in range(4):
        at = lax.rem(pos[2] + d, 4)
        outs[d][...] = jnp.where(
            at < 2,
            jnp.where(at == 0, parts[0], parts[1]),
            jnp.where(at == 2, parts[2], parts[3]),
        )


def place_kernel(pos, c0, c1, c2, c3, res):
    for d, c in enumerate((c0, c1, c2, c3)):
        head = pl.multiple_of(lax.rem(pos[2] + 4 - d, 4) * HEAD, HEAD)
        for j in range(2):
            res[:, j, pl.ds(head, HEAD)] = c[: res.shape[0], j * HEAD : (j + 1) * HEAD]


def on_device(tokens, tangent, w_query, w_key, value_weight, w_out):
    rows, width = tokens.shape
    seq = lax.axis_index("seq")
    core = lax.axis_index("mp")
    pos = jnp.stack([seq // 16, seq // 4 % 4, seq % 4, core]).astype(jnp.int32)
    piece_out = [out((4, rows, HEAD), BF)] * 4
    tok_in = (far_memory(), tokens)
    tan_in = (far_memory(), tangent)
    kv = flat_call(
        key_value_kernel,
        [None, tok_in, tan_in, (far_memory(), w_key), (far_memory(), value_weight)],
        piece_out,
        [
            pltpu.VMEM((2 * rows, width), BF),
            pltpu.VMEM((width, 1024), BF),
            pltpu.VMEM((2 * rows, 1024), F32),
            pltpu.VMEM((2 * rows, 1024), BF),
            pltpu.SemaphoreType.DMA((10,)),
        ],
        flops=2 * 256 * width * 1024,
        moved=2 * width * 1024,
        limit=62,
    )
    line, low, high = flat_call(
        join_kernel,
        [pos] + [(vmem(), c) for c in exchange(ring_y, kv)],
        [out((512, 512), BF), out((128, 512), BF), out((384, 512), BF)],
        moved=1 << 20,
    )
    passed = far_one(high)
    near = lines_on(line, 1)
    far_low = lines_on(low, 2)
    far_high = far_two(passed)
    lines = [far_low, far_high, near, line]
    q = flat_call(
        query_kernel,
        [pos, (vmem(), tokens), (vmem(), tangent), (vmem(), w_query)],
        [out((2, rows, 256), BF)] * 4,
        [pltpu.VMEM((2 * rows, width), BF)],
        flops=2 * 256 * width * 1024,
        moved=2 * width * 1024,
    )
    late_tokens, _ = lax.optimization_barrier((tokens, q[0]))
    q = exchange(ring_y, q)
    columns = late_tokens.T
    half = lax.dynamic_slice_in_dim(columns, core * (width // 2), width // 2, 0)
    (w_out,) = flat_call(
        load_kernel,
        [pos, (far_memory(), w_out)],
        [out(w_out.shape, BF)],
        [pltpu.SemaphoreType.DMA],
        moved=2 * w_out.size,
    )
    halves = exchange(ring_y, [half] * 4)[1:]
    partner_halves = [other_core(h) for h in halves]

    attended = flat_call(
        forward_kernel,
        [pos] + [(vmem(), a) for a in lines + q],
        [out((rows, 256), BF)] * 4 + [out((4, 256, HEAD), BF), out((4, 1152, 256), BF)],
        [pltpu.VMEM((4, 2, rows, 256), BF), pltpu.VMEM((4, rows, 256), BF)],
        flops=2 * 4 * 1152 * 256 * 128 * 5,
        moved=8 << 20,
        limit=24,
    )
    o, (q_all, p_all) = attended[:4], attended[4:]
    o = exchange(ring_y, o)
    small = whole((rows, 256))
    wide = pltpu.VMEM((rows, 1024), BF)
    total, sent = flat_call(
        out_kernel,
        [pos] + [(vmem(), a) for a in o] + [(vmem(), w_out)],
        [out((rows, width), F32), out((rows, width), BF)],
        [wide],
        flops=2 * rows * width * 1024,
        moved=2 * width * 1024,
    )
    other = other_core(sent)
    g = flat_call(
        gradient_kernel,
        [pos, (vmem(), total), (vmem(), other), (vmem(), w_out)],
        [out((rows, 256), BF)] * 4,
        [wide],
        flops=2 * rows * width * 1024,
        moved=2 * width * 1024,
    )
    g = exchange(ring_y, g)
    back = flat_call(
        backward_kernel,
        [pos] + [(vmem(), a) for a in g + lines + [q_all, p_all]],
        [out((rows, 256), BF)] * 4 + [out((512, 256), F32), out((512, 256), BF)] + [out((256, 256), BF)] * 2,
        [
            pltpu.VMEM((1536, HEAD), F32),
            pltpu.VMEM((1536, HEAD), F32),
            pltpu.VMEM((4, rows, 256), BF),
            pltpu.VMEM((4, rows, 256), BF),
        ],
        flops=2 * 4 * 1152 * 256 * 128 * 4,
        moved=6 << 20,
        limit=24,
    )
    dq, (own, to_near, to_low, to_high) = back[:4], back[4:]
    high = back_one(to_high)
    from_near = lines_on(to_near, -1)
    from_low = lines_on(to_low, -2)
    from_high = back_two(high)
    dq = exchange(ring_y, dq)
    pair = flat_call(
        pair_kernel,
        [pos] + [(vmem(), a) for a in (own, from_near, from_low, from_high)],
        [out((rows, 256), BF)] * 4,
        moved=1 << 20,
    )
    mixed_pair = exchange(ring_y, pair)

    part = (16 * PIECE, 256)
    (token_line,) = flat_call(
        token_kernel,
        [pos] + [(hbm(), a) for a in [columns] + halves + partner_halves],
        [out((width, 512), BF)],
        [pltpu.SemaphoreType.DMA((7,))],
        moved=5 << 20,
    )
    stage = flat_call(
        weight_kernel,
        [pos, (vmem(), token_line)] + [(vmem(), a) for a in pair],
        [out(part, BF)] * 4,
        flops=2 * 2688 * 512 * 256,
        moved=5 << 20,
    )
    stage = exchange(ring_x, stage)
    stage = flat_call(
        middle_kernel,
        [pos] + [(vmem(), v) for v in stage],
        [out((4 * PIECE, 256), BF)] * 4,
        [pltpu.VMEM((16 * PIECE, 256), F32)],
        moved=2 << 20,
    )
    stage = exchange(ring_z, stage)
    stage = flat_call(
        last_kernel,
        [pos] + [(vmem(), v) for v in stage],
        [out((PIECE, 256), F32)] * 4,
        moved=1 << 19,
    )
    stage = exchange(ring_y, stage)
    (weight_grad,) = call(
        place_kernel,
        (1,),
        [pos] + [(whole((PIECE, 256)), v) for v in stage],
        [out((width // 64, 2, 512), F32)],
        moved=1 << 18,
    )

    (base,) = flat_call(
        query_input_kernel,
        [pos] + [(vmem(), a) for a in dq] + [(vmem(), w_query)],
        [out((width, rows), F32)],
        [wide],
        flops=2 * rows * width * 1024,
        moved=2 * width * 1024,
    )
    narrow = pltpu.VMEM((rows, 512), BF)
    kept, given = flat_call(
        pair_input_kernel,
        [pos]
        + [(vmem(), c) for c in mixed_pair]
        + [(vmem(), base), (vmem(), w_key), (vmem(), value_weight)],
        [out((width // 2, rows), F32), out((width // 2, rows), BF)],
        [narrow, narrow, pltpu.VMEM((width, rows), F32)],
        flops=2 * rows * width * 1024,
        moved=2 * width * 1024,
    )
    theirs = other_core(given)
    input_grad = (kept + theirs.astype(F32)).astype(BF).T
    return input_grad, weight_grad


def solution(mesh):
    placed = (
        P("seq", None),
        P("seq", None),
        P(None, "mp"),
        P(None, "mp"),
        P(None, "mp"),
        P("mp", None),
    )
    return jax.shard_map(
        on_device,
        mesh=mesh,
        in_specs=placed,
        out_specs=(P("seq", "mp"), P("seq", None, "mp")),
        check_vma=False,
    )
```
